128 devices in a mesh: rows: 32 (over y, z, core), slab: 4 (over x).
Axes of the slice: x: 4, y: 4, z: 4, core: 2. Of those that a mesh axis runs over, the one named last changes fastest.
Arguments:
- snapshots: bfloat16 [262144, 2048], P(('rows', 'slab')), may hold values from -60 to 60
- start_block: float32 [2048, 64], replicated, may hold values from -6 to 6
- linear_op: float32 [64, 64], replicated, may hold values from -0.75 to 0.75
- quad_op: float32 [4096, 64], replicated, may hold values from -0.009765625 to 0.009765625
- offset: float32 [64], replicated, may hold values from -3 to 3
Outputs:
- projection: bfloat16 [262144, 64], P(('rows', 'slab'))
- reduced: float32 [2048, 64], P(('rows', 'slab'))
- mismatch: float32 [2048, 64], P(('rows', 'slab'))
The draws below stay inside these ranges and needn't reach their ends.
All inputs are finite; a program needn't handle non-finite values.
Results may differ from the reference program's by a relative error of at most 0.0029.
Values sent between devices are 32-bit elements; how exact they have to be, the bound alone decides.
No kernel may reach another device: no remote copies, remote signals or barrier semaphores. Data moves between devices by JAX's collectives and lax.ppermute only.
A program may use at most 128 MiB of HBM per device.

```python
import math
import jax
import jax.numpy as jnp
from jax import lax

K = 2048
RANK = 64
NROWS = 262144


def draw_snapshots(key, part):
    noise = jax.random.normal(key, (NROWS, K + 2), jnp.float32)
    mixed = noise[:, 2:] + 0.8 * noise[:, 1:-1] + 0.5 * noise[:, :-2]
    mixed = jnp.clip(mixed, -60.0, 60.0)
    return mixed.astype(jnp.bfloat16)


def bell_draw(rng, extent, scale, reach, kind=jnp.bfloat16):
    drawn = jax.random.normal(rng, extent, jnp.float32) * scale
    return jnp.minimum(jnp.maximum(drawn, -reach), reach).astype(kind)


def setup_inputs(seed: int = 0) -> dict:
    seeds = jax.random.split(jax.random.key(seed), 6)
    return {
        "snapshots": draw_snapshots(jax.random.fold_in(seeds[5], 71), 0),
        "start_block": bell_draw(seeds[1], (K, RANK), 1.0, 6.0, jnp.float32),
        "linear_op": bell_draw(seeds[2], (RANK, RANK), RANK ** -0.5, 0.75, jnp.float32),
        "quad_op": bell_draw(seeds[3], (RANK * RANK, RANK), (100 * RANK * RANK) ** -0.5, 0.009765625, jnp.float32),
        "offset": bell_draw(seeds[4], (RANK,), 0.5, 3.0, jnp.float32),
    }


def advance(state, linear_op, quad_op, offset):
    pairs = (state[:, :, None] * state[:, None, :]).reshape(state.shape[0], -1)
    hp = lax.Precision.HIGHEST
    change = jnp.dot(state, linear_op, precision=hp) + jnp.dot(pairs, quad_op, precision=hp) + offset[None, :]
    return state + 0.25 * change

def reference(snapshots, start_block, linear_op, quad_op, offset):
    hp = lax.Precision.HIGHEST
    total = snapshots.shape[0]
    width = snapshots.shape[1]
    block = math.gcd(total, 8192)
    pieces = snapshots.reshape(total // block, block, width)

    def power_step(acc, piece):
        floats = piece.astype(jnp.float32)
        inner = jnp.dot(floats, start_block, precision=hp)
        return (acc + jnp.dot(floats.T, inner, precision=hp), None)
    power, _ = lax.scan(power_step, jnp.zeros((width, RANK), jnp.float32), pieces)
    correlation = jnp.dot(power.T, power, precision=hp)
    factor = jnp.linalg.cholesky(correlation)
    basis = jax.scipy.linalg.solve_triangular(factor, power.T, lower=True).T

    def coord_step(acc, piece):
        floats = piece.astype(jnp.float32)
        modes = jnp.dot(floats, basis, precision=hp)
        return (acc + jnp.dot(floats.T, modes, precision=hp), modes.astype(jnp.bfloat16))
    coords, modes = lax.scan(coord_step, jnp.zeros((width, RANK), jnp.float32), pieces)
    projection = modes.reshape(total, RANK)
    reduced = coords * (math.sqrt(width) / total)
    state = advance(advance(reduced, linear_op, quad_op, offset), linear_op, quad_op, offset)
    target = jnp.concatenate([reduced[2:], jnp.zeros((2, RANK), jnp.float32)], axis=0)
    index = jnp.arange(width, dtype=jnp.int32)
    mismatch = jnp.where((index < width - 2)[:, None], state - target, jnp.float32(0.0))
    return (projection, reduced, mismatch)
```

```python
import math

import jax
import jax.numpy as jnp
from jax import lax
from jax.experimental import pallas as pl
from jax.experimental.pallas import tpu as pltpu
from jax.sharding import PartitionSpec as P

EVERY = ("rows", "slab")
RANK = 64
CHUNKS = 4
NT = (((1,), (1,)), ((), ()))
LIMIT = pltpu.CompilerParams(vmem_limit_bytes=48 * 1024 * 1024)
VMEM = pl.BlockSpec(memory_space=pltpu.VMEM)
ANY = pl.BlockSpec(memory_space=pl.ANY)


def three(value, axis):
    high = value.astype(jnp.bfloat16)
    rest = value - high.astype(jnp.float32)
    middle = rest.astype(jnp.bfloat16)
    low = (rest - middle.astype(jnp.float32)).astype(jnp.bfloat16)
    return jnp.concatenate([high, middle, low], axis=axis)


def fold(value, axis):
    if axis == 0:
        return value[:RANK] + value[RANK : 2 * RANK] + value[2 * RANK :]
    return value[:, :RANK] + value[:, RANK : 2 * RANK] + value[:, 2 * RANK :]


def fetches(source, buffer, sems):
    rows = source.shape[0] // CHUNKS
    return [
        pltpu.make_async_copy(
            source.at[pl.ds(i * rows, rows)], buffer.at[pl.ds(i * rows, rows)], sems.at[i]
        )
        for i in range(CHUNKS)
    ]


def power_kernel(x_hbm, start_ref, out_ref, x_ref, acc_ref, sems):
    copies = fetches(x_hbm, x_ref, sems)
    for copy in copies:
        copy.start()
    weights = three(start_ref[...], 0)
    rows = x_ref.shape[0] // CHUNKS
    for i, copy in enumerate(copies):
        copy.wait()
        x = x_ref[pl.ds(i * rows, rows), :]
        inner = fold(lax.dot_general(x, weights, NT, preferred_element_type=jnp.float32), 1)
        part = jnp.dot(three(inner.T, 0), x, preferred_element_type=jnp.float32)
        acc_ref[...] = part if i == 0 else acc_ref[...] + part
    power = fold(acc_ref[...], 0)
    wide = power.shape[1] // 128
    for i in range(out_ref.shape[0]):
        a, b = divmod(i, wide)
        out_ref[i] = power[8 * a : 8 * a + 8, 128 * b : 128 * b + 128]


def coords_kernel(x_hbm, power_ref, out_ref, modes_ref, corr_ref, x_ref, acc_ref, sems):
    copies = fetches(x_hbm, x_ref, sems)
    for copy in copies:
        copy.start()
    tall = RANK // 8
    wide = power_ref.shape[0] // tall
    power = jnp.concatenate(
        [
            jnp.concatenate([power_ref[a * wide + b] for b in range(wide)], axis=1)
            for a in range(tall)
        ],
        axis=0,
    )
    weights = three(power, 0)
    gram = lax.dot_general(weights, weights, NT, preferred_element_type=jnp.float32)
    corr_ref[...] = fold(fold(gram, 1), 0)
    rows = x_ref.shape[0] // CHUNKS
    for i, copy in enumerate(copies):
        copy.wait()
        x = x_ref[pl.ds(i * rows, rows), :]
        modes = fold(lax.dot_general(x, weights, NT, preferred_element_type=jnp.float32), 1)
        modes = modes.T
        modes_ref[:, pl.ds(i * rows, rows)] = modes
        part = jnp.dot(three(modes, 0), x, preferred_element_type=jnp.float32)
        acc_ref[...] = part if i == 0 else acc_ref[...] + part
    coords = fold(acc_ref[...], 0).T
    coords = coords.reshape(out_ref.shape[0], 2, 8, RANK)
    out_ref[...] = jnp.concatenate([coords[:, 0], coords[:, 1]], axis=-1)


def factor_kernel(corr_ref, modes_ref, projection_ref, inverse_ref):
    row = lax.broadcasted_iota(jnp.int32, (RANK, RANK), 0)
    column = lax.broadcasted_iota(jnp.int32, (RANK, RANK), 1)
    unit = jnp.where(row == column, jnp.float32(1.0), jnp.float32(0.0))
    work = jnp.concatenate([corr_ref[...], unit], axis=1)
    index = lax.broadcasted_iota(jnp.int32, (RANK, 1), 0)
    for k in range(RANK):
        pivot = work[k : k + 1, k : k + 1]
        scale = 1.0 / jnp.sqrt(pivot)
        line = work[k : k + 1, :] * scale
        multiplier = jnp.where(index > k, work[:, k : k + 1] * scale, 0.0)
        inverse_ref[k : k + 1, :] = line[:, RANK:]
        work = work - multiplier * line
    inverse = inverse_ref[...]
    modes = jnp.dot(
        inverse,
        modes_ref[...],
        precision=lax.Precision.HIGHEST,
        preferred_element_type=jnp.float32,
    )
    projection_ref[...] = modes.astype(jnp.bfloat16)


def advance(state, linear_op, quad_op, offset):
    pairs = (state[:, :, None] * state[:, None, :]).reshape(state.shape[0], -1)
    highest = lax.Precision.HIGHEST
    change = (
        jnp.dot(state, linear_op, precision=highest)
        + jnp.dot(pairs, quad_op, precision=highest)
        + offset[None, :]
    )
    return state + 0.25 * change


def exchanged_sum(parts):
    return jnp.sum(lax.all_to_all(parts, EVERY, 0, 0, tiled=True), axis=0)


def body(snapshots, start_block, linear_op, quad_op, offset):
    devices = lax.axis_size(EVERY)
    rows, width = snapshots.shape
    share = width // devices
    tile = (RANK * share // 128, 128)
    scratch = [
        pltpu.VMEM((rows, width), jnp.bfloat16),
        pltpu.VMEM((3 * RANK, width), jnp.float32),
        pltpu.SemaphoreType.DMA((CHUNKS,)),
    ]
    tiles = jax.ShapeDtypeStruct((devices, *tile), jnp.float32)
    parts = pl.pallas_call(
        power_kernel,
        out_shape=tiles,
        in_specs=[ANY, VMEM],
        out_specs=VMEM,
        scratch_shapes=scratch,
        compiler_params=LIMIT,
        name="power",
    )(snapshots, start_block.T)
    mine = exchanged_sum(parts)
    spread = jnp.broadcast_to(mine[None], (devices, *tile))
    power = lax.all_to_all(spread, EVERY, 0, 0, tiled=True)
    small = jax.ShapeDtypeStruct((RANK, RANK), jnp.float32)
    parts, modes, correlation = pl.pallas_call(
        coords_kernel,
        out_shape=(tiles, jax.ShapeDtypeStruct((RANK, rows), jnp.float32), small),
        in_specs=[ANY, VMEM],
        out_specs=(VMEM, VMEM, VMEM),
        scratch_shapes=scratch,
        compiler_params=LIMIT,
        name="coords",
    )(snapshots, power)
    packed = exchanged_sum(parts)
    projection, inverse = pl.pallas_call(
        factor_kernel,
        out_shape=(jax.ShapeDtypeStruct((RANK, rows), jnp.bfloat16), small),
        in_specs=[VMEM, VMEM],
        out_specs=(VMEM, VMEM),
        compiler_params=LIMIT,
        name="factor",
    )(correlation, modes)
    factor_scale = math.sqrt(width) / (rows * devices)
    highest = lax.Precision.HIGHEST
    coords = jnp.concatenate([packed[:, :RANK], packed[:, RANK:]], axis=0)
    reduced = lax.dot_general(coords, inverse, NT, precision=highest) * factor_scale
    state = advance(advance(reduced, linear_op, quad_op, offset), linear_op, quad_op, offset)
    route = [(i + 1, i) for i in range(devices - 1)]
    following = lax.ppermute(reduced[:2], EVERY, route)
    target = jnp.concatenate([reduced[2:], following], axis=0)
    position = lax.axis_index(EVERY) * share + jnp.arange(share, dtype=jnp.int32)
    mismatch = jnp.where((position < width - 2)[:, None], state - target, jnp.float32(0.0))
    return (projection.T, reduced, mismatch)


def solution(mesh):
    whole = P(EVERY, None)
    return jax.shard_map(
        body,
        mesh=mesh,
        in_specs=(whole, P(), P(), P(), P()),
        out_specs=(whole, whole, whole),
        check_vma=False,
    )
```

```python
import math

import jax
import jax.numpy as jnp
from jax import lax
from jax.experimental import pallas as pl
from jax.experimental.pallas import tpu as pltpu
from jax.sharding import PartitionSpec as P

EVERY = ("rows", "slab")
RANK = 64
CHUNKS = 4
NT = (((1,), (1,)), ((), ()))
LIMIT = pltpu.CompilerParams(vmem_limit_bytes=20 * 1024 * 1024)
VMEM = pl.BlockSpec(memory_space=pltpu.VMEM)
HBM = pl.BlockSpec(memory_space=pltpu.HBM)


def three(value):
    high = value.astype(jnp.bfloat16)
    rest = value - high.astype(jnp.float32)
    middle = rest.astype(jnp.bfloat16)
    low = (rest - middle.astype(jnp.float32)).astype(jnp.bfloat16)
    return jnp.concatenate([high, middle, low], axis=0)


def fold_rows(value):
    third = value.shape[0] // 3
    return value[:third] + value[third : 2 * third] + value[2 * third :]


def fold_lanes(value):
    third = value.shape[1] // 3
    return value[:, :third] + value[:, third : 2 * third] + value[:, 2 * third :]


def dot_nt(left, right):
    return lax.dot_general(left, right, NT, preferred_element_type=jnp.float32)


def passes(weights, block, ready, acc_ref, keep):
    held = None
    for i in range(CHUNKS):
        ready(i)
        inner = fold_rows(dot_nt(weights, block(i)))
        if held is not None:
            part = jnp.dot(held, block(i - 1), preferred_element_type=jnp.float32)
            acc_ref[...] = part if i == 1 else acc_ref[...] + part
        keep(i, inner)
        held = three(inner)
    part = jnp.dot(held, block(CHUNKS - 1), preferred_element_type=jnp.float32)
    return fold_rows(acc_ref[...] + part)


def power_kernel(x_hbm, start_hbm, out_ref, x_ref, start_ref, acc_ref, sems):
    rows = x_ref.shape[0] // CHUNKS
    first = pltpu.make_async_copy(start_hbm, start_ref, sems.at[CHUNKS])
    first.start()
    copies = [
        pltpu.make_async_copy(
            x_hbm.at[pl.ds(i * rows, rows)], x_ref.at[pl.ds(i * rows, rows)], sems.at[i]
        )
        for i in range(CHUNKS)
    ]
    for copy in copies:
        copy.start()
    first.wait()
    weights = three(start_ref[...])
    power = passes(
        weights,
        lambda i: x_ref[pl.ds(i * rows, rows), :],
        lambda i: copies[i].wait(),
        acc_ref,
        lambda i, inner: None,
    )
    wide = power.shape[1] // 128
    for i in range(out_ref.shape[0]):
        a, b = divmod(i, wide)
        out_ref[i] = power[8 * a : 8 * a + 8, 128 * b : 128 * b + 128]


def spread_kernel(parts_ref, out_ref):
    out_ref[...] = jnp.broadcast_to(jnp.sum(parts_ref[...], axis=0)[None], out_ref.shape)


def coords_kernel(x_ref, power_ref, out_ref, modes_ref, corr_ref, acc_ref):
    rows = x_ref.shape[0] // CHUNKS
    tall = RANK // 8
    wide = power_ref.shape[0] // tall
    power = jnp.concatenate(
        [
            jnp.concatenate([power_ref[a * wide + b] for b in range(wide)], axis=1)
            for a in range(tall)
        ],
        axis=0,
    )
    weights = three(power)

    def keep(i, inner):
        modes_ref[:, pl.ds(i * rows, rows)] = inner

    coords = passes(
        weights, lambda i: x_ref[pl.ds(i * rows, rows), :], lambda i: None, acc_ref, keep
    ).T
    coords = coords.reshape(out_ref.shape[0], 2, 8, RANK)
    out_ref[...] = jnp.concatenate([coords[:, 0], coords[:, 1]], axis=-1)
    corr_ref[...] = fold_rows(fold_lanes(dot_nt(weights, weights)))


def factor_kernel(corr_ref, modes_ref, quad_ref, projection_ref, inverse_ref, pieces_ref):
    pieces_ref[...] = three(quad_ref[...])
    row = lax.broadcasted_iota(jnp.int32, (RANK, RANK), 0)
    column = lax.broadcasted_iota(jnp.int32, (RANK, RANK), 1)
    unit = jnp.where(row == column, jnp.float32(1.0), jnp.float32(0.0))
    work = jnp.concatenate([corr_ref[...], unit], axis=1)
    index = lax.broadcasted_iota(jnp.int32, (RANK, 1), 0)
    for k in range(RANK):
        line = work[k : k + 1, :]
        pivot = line[:, k : k + 1]
        inverse_ref[k : k + 1, :] = line[:, RANK:] * (1.0 / jnp.sqrt(pivot))
        multiplier = jnp.where(index > k, work[:, k : k + 1], 0.0)
        work = work - multiplier * (line * (1.0 / pivot))
    inverse = inverse_ref[...]
    modes = jnp.dot(
        inverse,
        modes_ref[...],
        precision=lax.Precision.HIGHEST,
        preferred_element_type=jnp.float32,
    )
    projection_ref[...] = modes.astype(jnp.bfloat16)


def reduced_kernel(scale, parts_ref, inverse_ref, out_ref, keep_ref, head_ref):
    packed = jnp.sum(parts_ref[...], axis=0)
    coords = jnp.concatenate([packed[:, :RANK], packed[:, RANK:]], axis=0)
    reduced = scale * lax.dot_general(
        coords,
        inverse_ref[...],
        NT,
        precision=lax.Precision.HIGHEST,
        preferred_element_type=jnp.float32,
    )
    out_ref[...] = reduced
    keep_ref[...] = reduced
    head_ref[...] = reduced[:2]


def rollout_kernel(reduced_ref, linear_ref, pieces_ref, offset_ref, out_ref):
    state = reduced_ref[...]
    pieces = pieces_ref[...]
    upper = lax.broadcasted_iota(jnp.int32, (state.shape[0], 2 * RANK), 1) >= RANK
    for _ in range(2):
        twice = jnp.concatenate([state, state], axis=1)
        pairs = jnp.concatenate(
            [
                jnp.where(upper, state[:, 2 * i + 1 : 2 * i + 2], state[:, 2 * i : 2 * i + 1])
                * twice
                for i in range(RANK // 2)
            ],
            axis=1,
        )
        quadratic = fold_rows(fold_lanes(dot_nt(three(pairs), pieces)))
        linear = jnp.dot(
            state,
            linear_ref[...],
            precision=lax.Precision.HIGHEST,
            preferred_element_type=jnp.float32,
        )
        state = state + 0.25 * (linear + quadratic + offset_ref[...])
    out_ref[...] = state


def in_hbm(value):
    return pltpu.with_memory_space_constraint(value, pltpu.HBM)


def call(kernel, name, outs, ins, scratch=()):
    return pl.pallas_call(
        kernel,
        out_shape=outs,
        in_specs=ins,
        out_specs=jax.tree.map(lambda _: VMEM, outs),
        scratch_shapes=list(scratch),
        compiler_params=LIMIT,
        name=name,
    )


def body(snapshots, start_block, linear_op, quad_op, offset):
    devices = lax.axis_size(EVERY)
    rows, width = snapshots.shape
    share = width // devices
    f32 = jnp.float32
    shape = jax.ShapeDtypeStruct
    tiles = shape((devices, RANK * share // 128, 128), f32)
    small = shape((RANK, RANK), f32)
    own = shape((share, RANK), f32)
    acc = pltpu.VMEM((3 * RANK, width), f32)
    parts, held = call(
        power_kernel,
        "power",
        (tiles, shape((rows, width), jnp.bfloat16)),
        [HBM, HBM],
        [
            pltpu.VMEM((RANK, width), f32),
            acc,
            pltpu.SemaphoreType.DMA((CHUNKS + 1,)),
        ],
    )(in_hbm(snapshots), in_hbm(start_block.T))
    parts = lax.all_to_all(parts, EVERY, 0, 0, tiled=True)
    spread = call(spread_kernel, "spread", tiles, [VMEM])(parts)
    power = lax.all_to_all(spread, EVERY, 0, 0, tiled=True)
    parts, modes, correlation = call(
        coords_kernel,
        "coords",
        (tiles, shape((RANK, rows), f32), small),
        [VMEM, VMEM],
        [acc],
    )(held, power)
    parts = lax.all_to_all(parts, EVERY, 0, 0, tiled=True)
    projection, inverse, pieces = call(
        factor_kernel,
        "factor",
        (shape((RANK, rows), jnp.bfloat16), small, shape((3 * RANK, RANK * RANK), jnp.bfloat16)),
        [VMEM, VMEM, VMEM],
    )(correlation, modes, quad_op.T)
    factor_scale = math.sqrt(width) / (rows * devices)
    reduced, kept, head = call(
        lambda *refs: reduced_kernel(factor_scale, *refs),
        "reduced",
        (own, own, shape((2, RANK), f32)),
        [VMEM, VMEM],
    )(parts, inverse)
    route = [(i + 1, i) for i in range(devices - 1)]
    following = lax.ppermute(head, EVERY, route)
    state = call(rollout_kernel, "rollout", own, [VMEM] * 4)(
        kept, linear_op, pieces, offset[None, :]
    )
    target = jnp.concatenate([kept[2:], following], axis=0)
    position = lax.axis_index(EVERY) * share + jnp.arange(share, dtype=jnp.int32)
    mismatch = jnp.where((position < width - 2)[:, None], state - target, jnp.float32(0.0))
    return (projection.T, reduced, mismatch)


def solution(mesh):
    whole = P(EVERY, None)
    return jax.shard_map(
        body,
        mesh=mesh,
        in_specs=(whole, P(), P(), P(), P()),
        out_specs=(whole, whole, whole),
        check_vma=False,
    )
```

```python
import math

import jax
import jax.numpy as jnp
from jax import lax
from jax.experimental import pallas as pl
from jax.experimental.pallas import tpu as pltpu
from jax.sharding import Mesh
from jax.sharding import PartitionSpec as P

EVERY = ("yz", "core", "slab")
CHIPS = ("yz", "slab")
CORES = 2
RANK = 64
CHUNKS = 4
NT = (((1,), (1,)), ((), ()))
LIMIT = pltpu.CompilerParams(vmem_limit_bytes=20 * 1024 * 1024)
SMEM = pl.BlockSpec(memory_space=pltpu.SMEM)
VMEM = pl.BlockSpec(memory_space=pltpu.VMEM)
HBM = pl.BlockSpec(memory_space=pltpu.HBM)


def three(value):
    high = value.astype(jnp.bfloat16)
    rest = value - high.astype(jnp.float32)
    middle = rest.astype(jnp.bfloat16)
    low = (rest - middle.astype(jnp.float32)).astype(jnp.bfloat16)
    return jnp.concatenate([high, middle, low], axis=0)


def fold_rows(value):
    third = value.shape[0] // 3
    return value[:third] + value[third : 2 * third] + value[2 * third :]


def fold_lanes(value):
    third = value.shape[1] // 3
    return value[:, :third] + value[:, third : 2 * third] + value[:, 2 * third :]


def dot_nt(left, right):
    return lax.dot_general(left, right, NT, preferred_element_type=jnp.float32)


def passes(weights, block, ready, acc_ref, keep):
    held = None
    for i in range(CHUNKS):
        ready(i)
        inner = fold_rows(dot_nt(weights, block(i)))
        if held is not None:
            part = jnp.dot(held, block(i - 1), preferred_element_type=jnp.float32)
            acc_ref[...] = part if i == 1 else acc_ref[...] + part
        keep(i, inner)
        held = three(inner)
    part = jnp.dot(held, block(CHUNKS - 1), preferred_element_type=jnp.float32)
    return fold_rows(acc_ref[...] + part)


def power_kernel(x_hbm, start_hbm, out_ref, x_ref, start_ref, acc_ref, sems):
    rows = x_ref.shape[0] // CHUNKS
    first = pltpu.make_async_copy(start_hbm, start_ref, sems.at[CHUNKS])
    first.start()
    copies = [
        pltpu.make_async_copy(
            x_hbm.at[pl.ds(i * rows, rows)], x_ref.at[pl.ds(i * rows, rows)], sems.at[i]
        )
        for i in range(CHUNKS)
    ]
    for copy in copies:
        copy.start()
    first.wait()
    weights = three(start_ref[...])
    power = passes(
        weights,
        lambda i: x_ref[pl.ds(i * rows, rows), :],
        lambda i: copies[i].wait(),
        acc_ref,
        lambda i, inner: None,
    )
    wide = power.shape[1] // 128
    for i in range(out_ref.shape[0]):
        a, b = divmod(i, wide)
        out_ref[i] = power[8 * a : 8 * a + 8, 128 * b : 128 * b + 128]


def spread_kernel(parts_ref, out_ref):
    out_ref[...] = jnp.broadcast_to(jnp.sum(parts_ref[...], axis=0)[None], out_ref.shape)


def whole_power(power_ref):
    tall = RANK // 8
    wide = power_ref.shape[0] // tall
    rows = [
        jnp.concatenate([power_ref[a * wide + b] for b in range(wide)], axis=1)
        for a in range(tall)
    ]
    return jnp.concatenate(rows, axis=0)


def coords_kernel(core_ref, x_ref, power_ref, keep_ref, send_ref, modes_ref, acc_ref):
    rows = x_ref.shape[0] // CHUNKS
    weights = three(whole_power(power_ref))

    def store(i, inner):
        modes_ref[:, pl.ds(i * rows, rows)] = inner

    coords = passes(
        weights, lambda i: x_ref[pl.ds(i * rows, rows), :], lambda i: None, acc_ref, store
    ).T
    groups, deep, _ = keep_ref.shape
    coords = coords.reshape(groups, coords.shape[0] // groups, RANK)
    after = jnp.concatenate([coords[1:, :8], coords[:1, :8]], axis=0)
    coords = jnp.concatenate([coords, after], axis=1)
    half = deep - 8
    packed = [
        jnp.concatenate(
            [coords[:, 2 * half * c : 2 * half * c + deep], coords[:, 2 * half * c + half :][:, :deep]],
            axis=-1,
        )
        for c in range(CORES)
    ]
    first = core_ref[0] == 0
    keep_ref[...] = jnp.where(first, packed[0], packed[1])
    send_ref[...] = jnp.where(first, packed[1], packed[0])


def prepare_kernel(power_ref, quad_ref, corr_ref, pieces_ref):
    pieces_ref[...] = three(quad_ref[...])
    weights = three(whole_power(power_ref))
    corr_ref[...] = fold_rows(fold_lanes(dot_nt(weights, weights)))


def pair_kernel(keep_ref, came_ref, out_ref):
    total = keep_ref[...] + came_ref[...]
    groups = total.shape[0]
    chips, share, _ = out_ref.shape
    slabs = chips // groups
    chunks = []
    for x in range(slabs):
        side, place = divmod(x * share, total.shape[1] - 8)
        rows = total[:, place : place + share + 8, side * RANK : (side + 1) * RANK]
        chunks.append(jnp.concatenate([rows[:, :share], rows[:, 2 : share + 2]], axis=-1))
    out_ref[...] = jnp.stack(chunks, axis=1).reshape(out_ref.shape)


def factor_kernel(corr_ref, modes_hbm, projection_ref, inverse_ref, modes_ref, sem):
    fetch = pltpu.make_async_copy(modes_hbm, modes_ref, sem)
    fetch.start()
    row = lax.broadcasted_iota(jnp.int32, (RANK, RANK), 0)
    column = lax.broadcasted_iota(jnp.int32, (RANK, RANK), 1)
    unit = jnp.where(row == column, jnp.float32(1.0), jnp.float32(0.0))
    work = jnp.concatenate([corr_ref[...], unit], axis=1)
    index = lax.broadcasted_iota(jnp.int32, (RANK, 1), 0)
    for k in range(RANK):
        line = work[k : k + 1, :]
        pivot = line[:, k : k + 1]
        inverse_ref[k : k + 1, :] = line[:, RANK:] * (1.0 / jnp.sqrt(pivot))
        multiplier = jnp.where(index > k, work[:, k : k + 1], 0.0)
        work = work - multiplier * (line * (1.0 / pivot))
    fetch.wait()
    modes = jnp.dot(
        inverse_ref[...],
        modes_ref[...],
        precision=lax.Precision.HIGHEST,
        preferred_element_type=jnp.float32,
    )
    projection_ref[...] = modes.astype(jnp.bfloat16)


def rollout_kernel(
    scale, width, place_ref, parts_ref, inverse_ref, linear_ref, pieces_ref, offset_ref,
    reduced_ref, mismatch_ref,
):
    packed = jnp.sum(parts_ref[...], axis=0)
    share = packed.shape[0]
    coords = jnp.concatenate([packed[:, :RANK], packed[:, RANK:]], axis=0)
    coords = scale * lax.dot_general(
        coords,
        inverse_ref[...],
        NT,
        precision=lax.Precision.HIGHEST,
        preferred_element_type=jnp.float32,
    )
    state, target = coords[:share], coords[share:]
    reduced_ref[...] = state
    pieces = pieces_ref[...]
    upper = lax.broadcasted_iota(jnp.int32, (share, 2 * RANK), 1) >= RANK
    for _ in range(2):
        twice = jnp.concatenate([state, state], axis=1)
        pairs = jnp.concatenate(
            [
                jnp.where(upper, state[:, 2 * i + 1 : 2 * i + 2], state[:, 2 * i : 2 * i + 1])
                * twice
                for i in range(RANK // 2)
            ],
            axis=1,
        )
        quadratic = fold_rows(fold_lanes(dot_nt(three(pairs), pieces)))
        linear = jnp.dot(
            state,
            linear_ref[...],
            precision=lax.Precision.HIGHEST,
            preferred_element_type=jnp.float32,
        )
        state = state + 0.25 * (linear + quadratic + offset_ref[...])
    position = place_ref[0] * share + lax.broadcasted_iota(jnp.int32, (share, 1), 0)
    mismatch_ref[...] = jnp.where(position < width - 2, state - target, jnp.float32(0.0))


def in_hbm(value):
    return pltpu.with_memory_space_constraint(value, pltpu.HBM)


def call(kernel, name, outs, ins, scratch=()):
    return pl.pallas_call(
        kernel,
        out_shape=outs,
        in_specs=ins,
        out_specs=jax.tree.map(lambda _: VMEM, outs),
        scratch_shapes=list(scratch),
        compiler_params=LIMIT,
        name=name,
    )


def body(snapshots, start_block, linear_op, quad_op, offset):
    devices = lax.axis_size(EVERY)
    rows, width = snapshots.shape
    share = width // devices
    f32 = jnp.float32
    shape = jax.ShapeDtypeStruct
    tiles = shape((devices, RANK * share // 128, 128), f32)
    small = shape((RANK, RANK), f32)
    own = shape((share, RANK), f32)
    acc = pltpu.VMEM((3 * RANK, width), f32)
    core, place = lax.axis_index("core")[None], lax.axis_index(EVERY)[None]
    start_block, core, place = lax.optimization_barrier((start_block, core, place))
    parts, held = call(
        power_kernel,
        "power",
        (tiles, shape((rows, width), jnp.bfloat16)),
        [HBM, HBM],
        [
            pltpu.VMEM((RANK, width), f32),
            acc,
            pltpu.SemaphoreType.DMA((CHUNKS + 1,)),
        ],
    )(in_hbm(snapshots), in_hbm(start_block.T))
    parts = lax.all_to_all(parts, EVERY, 0, 0, tiled=True)
    spread = call(spread_kernel, "spread", tiles, [VMEM])(parts)
    power = lax.all_to_all(spread, EVERY, 0, 0, tiled=True)
    groups = lax.axis_size("yz")
    deep = width // groups // CORES // 2 + 8
    packed = shape((groups, deep, 2 * RANK), f32)
    keep, send, modes = call(
        coords_kernel,
        "coords",
        (packed, packed, shape((RANK, rows), f32)),
        [SMEM, VMEM, VMEM],
        [acc],
    )(core, held, power)
    came = lax.ppermute(send, "core", [(0, 1), (1, 0)])
    correlation, pieces = call(
        prepare_kernel,
        "prepare",
        (small, shape((3 * RANK, RANK * RANK), jnp.bfloat16)),
        [VMEM, VMEM],
    )(power, quad_op.T)
    came, correlation, pieces = lax.optimization_barrier((came, correlation, pieces))
    chunks = shape((devices // CORES, share, 2 * RANK), f32)
    parts = call(pair_kernel, "pair", chunks, [VMEM, VMEM])(keep, came)
    parts = lax.all_to_all(parts, CHIPS, 0, 0, tiled=True)
    projection, inverse = call(
        factor_kernel,
        "factor",
        (shape((RANK, rows), jnp.bfloat16), small),
        [VMEM, HBM],
        [pltpu.VMEM((RANK, rows), f32), pltpu.SemaphoreType.DMA(())],
    )(correlation, in_hbm(modes))
    factor_scale = math.sqrt(width) / (rows * devices)
    reduced, mismatch = call(
        lambda *refs: rollout_kernel(factor_scale, width, *refs),
        "rollout",
        (own, own),
        [SMEM] + [VMEM] * 5,
    )(place, parts, inverse, linear_op, pieces, offset[None, :])
    return (projection.T, reduced, mismatch)


def solution(mesh):
    slabs = mesh.shape["slab"]
    split = Mesh(mesh.devices.reshape(-1, CORES, slabs), EVERY)
    whole = P(EVERY, None)
    return jax.shard_map(
        body,
        mesh=split,
        in_specs=(whole, P(), P(), P(), P()),
        out_specs=(whole, whole, whole),
        check_vma=False,
    )
```

```python
import math

import jax
import jax.numpy as jnp
from jax import lax
from jax.experimental import pallas as pl
from jax.experimental.pallas import tpu as pltpu
from jax.sharding import Mesh
from jax.sharding import PartitionSpec as P

EVERY = ("yz", "core", "slab")
CHIPS = ("yz", "slab")
CORES = 2
RANK = 64
CHUNKS = 4
NT = (((1,), (1,)), ((), ()))
LIMIT = pltpu.CompilerParams(vmem_limit_bytes=20 * 1024 * 1024)
SMEM = pl.BlockSpec(memory_space=pltpu.SMEM)
VMEM = pl.BlockSpec(memory_space=pltpu.VMEM)
HBM = pl.BlockSpec(memory_space=pltpu.HBM)


def three(value):
    high = value.astype(jnp.bfloat16)
    rest = value - high.astype(jnp.float32)
    middle = rest.astype(jnp.bfloat16)
    low = (rest - middle.astype(jnp.float32)).astype(jnp.bfloat16)
    return jnp.concatenate([high, middle, low], axis=0)


def fold_rows(value):
    third = value.shape[0] // 3
    return value[:third] + value[third : 2 * third] + value[2 * third :]


def fold_lanes(value):
    third = value.shape[1] // 3
    return value[:, :third] + value[:, third : 2 * third] + value[:, 2 * third :]


def dot_nt(left, right):
    return lax.dot_general(left, right, NT, preferred_element_type=jnp.float32)


def passes(inner, block, count, acc_ref):
    held = None
    for i in range(count):
        value = inner(i)
        if held is not None:
            part = jnp.dot(held, block(i - 1), preferred_element_type=jnp.float32)
            acc_ref[...] = part if i == 1 else acc_ref[...] + part
        held = three(value)
    part = jnp.dot(held, block(count - 1), preferred_element_type=jnp.float32)
    return fold_rows(acc_ref[...] + part)


def put_tiles(out_ref, value):
    wide = value.shape[1] // 128
    for i in range(out_ref.shape[0]):
        a, b = divmod(i, wide)
        out_ref[i] = value[8 * a : 8 * a + 8, 128 * b : 128 * b + 128]


def get_tiles(ref):
    tall = RANK // 8
    wide = ref.shape[0] // tall
    rows = [
        jnp.concatenate([ref[a * wide + b] for b in range(wide)], axis=1) for a in range(tall)
    ]
    return jnp.concatenate(rows, axis=0)


def power_kernel(core_ref, x_hbm, start_hbm, send_ref, x_ref, inner_ref, start_ref, acc_ref, sems):
    half = x_ref.shape[1] // CORES
    rows = x_ref.shape[0] // CHUNKS
    copies = []
    for k in range(CORES):
        source = pl.multiple_of(half * jnp.bitwise_xor(core_ref[0], k), half)
        there, here = pl.ds(source, half), pl.ds(k * half, half)
        copies.append(
            [pltpu.make_async_copy(start_hbm.at[:, there], start_ref.at[:, here], sems.at[k, CHUNKS])]
            + [
                pltpu.make_async_copy(
                    x_hbm.at[pl.ds(i * rows, rows), there],
                    x_ref.at[pl.ds(i * rows, rows), here],
                    sems.at[k, i],
                )
                for i in range(CHUNKS)
            ]
        )
    for pair in zip(*copies):
        for copy in pair:
            copy.start()
    for k in range(CORES):
        copies[k][0].wait()
    weights = three(start_ref[...])

    def inner(i):
        for k in range(CORES):
            copies[k][i + 1].wait()
        value = fold_rows(dot_nt(weights, x_ref[pl.ds(i * rows, rows), :]))
        inner_ref[:, pl.ds(i * rows, rows)] = three(value)
        return value

    put_tiles(
        send_ref,
        passes(inner, lambda i: x_ref[pl.ds(i * rows, rows), half:], CHUNKS, acc_ref),
    )


def own_power_kernel(inner_ref, x_ref, keep_ref):
    half = x_ref.shape[1] // CORES
    put_tiles(
        keep_ref,
        fold_rows(jnp.dot(inner_ref[...], x_ref[:, :half], preferred_element_type=jnp.float32)),
    )


def add_kernel(keep_ref, came_ref, out_ref):
    out_ref[...] = keep_ref[...] + came_ref[...]


def spread_kernel(parts_ref, out_ref):
    out_ref[...] = jnp.broadcast_to(jnp.sum(parts_ref[...], axis=0)[None], out_ref.shape)


def own_modes_kernel(x_ref, own_ref, modes_ref):
    half = x_ref.shape[1] // CORES
    modes_ref[...] = fold_rows(dot_nt(three(get_tiles(own_ref)), x_ref[:, :half]))


def coords_kernel(core_ref, x_ref, own_modes_ref, other_ref, keep_ref, send_ref, modes_ref, acc_ref):
    half = x_ref.shape[1] // CORES
    rows = x_ref.shape[0] // CHUNKS
    weights = three(get_tiles(other_ref))

    def inner(i):
        here = pl.ds(i * rows, rows)
        value = own_modes_ref[:, here] + fold_rows(dot_nt(weights, x_ref[here, half:]))
        modes_ref[:, here] = value
        return value

    coords = passes(inner, lambda i: x_ref[pl.ds(i * rows, rows), :], CHUNKS, acc_ref).T
    first = core_ref[0] == 0
    own, other = coords[:half], coords[half:]
    coords = jnp.concatenate([jnp.where(first, own, other), jnp.where(first, other, own)], axis=0)
    groups, deep, _ = keep_ref.shape
    coords = coords.reshape(groups, coords.shape[0] // groups, RANK)
    after = jnp.concatenate([coords[1:, :8], coords[:1, :8]], axis=0)
    coords = jnp.concatenate([coords, after], axis=1)
    span = deep - 8
    packed = [
        jnp.concatenate(
            [coords[:, 2 * span * c : 2 * span * c + deep], coords[:, 2 * span * c + span :][:, :deep]],
            axis=-1,
        )
        for c in range(CORES)
    ]
    keep_ref[...] = jnp.where(first, packed[0], packed[1])
    send_ref[...] = jnp.where(first, packed[1], packed[0])


def prepare_kernel(own_ref, other_ref, quad_ref, corr_ref, pieces_ref):
    pieces_ref[...] = three(quad_ref[...])
    power = jnp.concatenate([get_tiles(own_ref), get_tiles(other_ref)], axis=1)
    weights = three(power)
    corr_ref[...] = fold_rows(fold_lanes(dot_nt(weights, weights)))


def pair_kernel(keep_ref, came_ref, out_ref):
    total = keep_ref[...] + came_ref[...]
    groups = total.shape[0]
    chips, share, _ = out_ref.shape
    slabs = chips // groups
    chunks = []
    for x in range(slabs):
        side, place = divmod(x * share, total.shape[1] - 8)
        rows = total[:, place : place + share + 8, side * RANK : (side + 1) * RANK]
        chunks.append(jnp.concatenate([rows[:, :share], rows[:, 2 : share + 2]], axis=-1))
    out_ref[...] = jnp.stack(chunks, axis=1).reshape(out_ref.shape)


def factor_kernel(corr_ref, modes_hbm, projection_ref, inverse_ref, modes_ref, sem):
    fetch = pltpu.make_async_copy(modes_hbm, modes_ref, sem)
    fetch.start()
    row = lax.broadcasted_iota(jnp.int32, (RANK, RANK), 0)
    column = lax.broadcasted_iota(jnp.int32, (RANK, RANK), 1)
    unit = jnp.where(row == column, jnp.float32(1.0), jnp.float32(0.0))
    work = jnp.concatenate([corr_ref[...], unit], axis=1)
    index = lax.broadcasted_iota(jnp.int32, (RANK, 1), 0)
    for k in range(RANK):
        line = work[k : k + 1, :]
        pivot = line[:, k : k + 1]
        inverse_ref[k : k + 1, :] = line[:, RANK:] * (1.0 / jnp.sqrt(pivot))
        multiplier = jnp.where(index > k, work[:, k : k + 1], 0.0)
        work = work - multiplier * (line * (1.0 / pivot))
    fetch.wait()
    modes = jnp.dot(
        inverse_ref[...],
        modes_ref[...],
        precision=lax.Precision.HIGHEST,
        preferred_element_type=jnp.float32,
    )
    projection_ref[...] = modes.astype(jnp.bfloat16)


def rollout_kernel(
    scale, width, place_ref, parts_ref, inverse_ref, linear_ref, pieces_ref, offset_ref,
    reduced_ref, mismatch_ref,
):
    packed = jnp.sum(parts_ref[...], axis=0)
    share = packed.shape[0]
    coords = jnp.concatenate([packed[:, :RANK], packed[:, RANK:]], axis=0)
    coords = scale * lax.dot_general(
        coords,
        inverse_ref[...],
        NT,
        precision=lax.Precision.HIGHEST,
        preferred_element_type=jnp.float32,
    )
    state, target = coords[:share], coords[share:]
    reduced_ref[...] = state
    pieces = pieces_ref[...]
    upper = lax.broadcasted_iota(jnp.int32, (share, 2 * RANK), 1) >= RANK
    for _ in range(2):
        twice = jnp.concatenate([state, state], axis=1)
        pairs = jnp.concatenate(
            [
                jnp.where(upper, state[:, 2 * i + 1 : 2 * i + 2], state[:, 2 * i : 2 * i + 1])
                * twice
                for i in range(RANK // 2)
            ],
            axis=1,
        )
        quadratic = fold_rows(fold_lanes(dot_nt(three(pairs), pieces)))
        linear = jnp.dot(
            state,
            linear_ref[...],
            precision=lax.Precision.HIGHEST,
            preferred_element_type=jnp.float32,
        )
        state = state + 0.25 * (linear + quadratic + offset_ref[...])
    position = place_ref[0] * share + lax.broadcasted_iota(jnp.int32, (share, 1), 0)
    mismatch_ref[...] = jnp.where(position < width - 2, state - target, jnp.float32(0.0))


def in_hbm(value):
    return pltpu.with_memory_space_constraint(value, pltpu.HBM)


def call(kernel, name, outs, ins, scratch=()):
    return pl.pallas_call(
        kernel,
        out_shape=outs,
        in_specs=ins,
        out_specs=jax.tree.map(lambda _: VMEM, outs),
        scratch_shapes=list(scratch),
        compiler_params=LIMIT,
        name=name,
    )


def body(snapshots, start_block, linear_op, quad_op, offset):
    devices = lax.axis_size(EVERY)
    rows, width = snapshots.shape
    share = width // devices
    f32 = jnp.float32
    shape = jax.ShapeDtypeStruct
    chips = devices // CORES
    tiles = shape((chips, RANK * share // 128, 128), f32)
    small = shape((RANK, RANK), f32)
    own = shape((share, RANK), f32)
    core, place = lax.axis_index("core")[None], lax.axis_index(EVERY)[None]
    start_block, core, place = lax.optimization_barrier((start_block, core, place))
    send, held, inner = call(
        power_kernel,
        "power",
        (
            tiles,
            shape((rows, width), jnp.bfloat16),
            shape((3 * RANK, rows), jnp.bfloat16),
        ),
        [SMEM, HBM, HBM],
        [
            pltpu.VMEM((RANK, width), f32),
            pltpu.VMEM((3 * RANK, width // CORES), f32),
            pltpu.SemaphoreType.DMA((CORES, CHUNKS + 1)),
        ],
    )(core, in_hbm(snapshots), in_hbm(start_block.T))
    swap = [(0, 1), (1, 0)]
    came = lax.ppermute(send, "core", swap)
    keep = call(own_power_kernel, "own_power", tiles, [VMEM, VMEM])(inner, held)
    parts = call(add_kernel, "add", tiles, [VMEM, VMEM])(keep, came)
    parts = lax.all_to_all(parts, CHIPS, 0, 0, tiled=True)
    spread = call(spread_kernel, "spread", tiles, [VMEM])(parts)
    mine = lax.all_to_all(spread, CHIPS, 0, 0, tiled=True)
    theirs = lax.ppermute(mine, "core", swap)
    own_modes = call(own_modes_kernel, "own_modes", shape((RANK, rows), f32), [VMEM, VMEM])(
        held, mine
    )
    groups = lax.axis_size("yz")
    deep = width // groups // CORES // 2 + 8
    packed = shape((groups, deep, 2 * RANK), f32)
    keep, send, modes = call(
        coords_kernel,
        "coords",
        (packed, packed, shape((RANK, rows), f32)),
        [SMEM, VMEM, VMEM, VMEM],
        [pltpu.VMEM((3 * RANK, width), f32)],
    )(core, held, own_modes, theirs)
    came = lax.ppermute(send, "core", swap)
    correlation, pieces = call(
        prepare_kernel,
        "prepare",
        (small, shape((3 * RANK, RANK * RANK), jnp.bfloat16)),
        [VMEM, VMEM, VMEM],
    )(mine, theirs, quad_op.T)
    came, correlation, pieces = lax.optimization_barrier((came, correlation, pieces))
    chunks = shape((chips, share, 2 * RANK), f32)
    parts = call(pair_kernel, "pair", chunks, [VMEM, VMEM])(keep, came)
    parts = lax.all_to_all(parts, CHIPS, 0, 0, tiled=True)
    projection, inverse = call(
        factor_kernel,
        "factor",
        (shape((RANK, rows), jnp.bfloat16), small),
        [VMEM, HBM],
        [pltpu.VMEM((RANK, rows), f32), pltpu.SemaphoreType.DMA(())],
    )(correlation, in_hbm(modes))
    factor_scale = math.sqrt(width) / (rows * devices)
    reduced, mismatch = call(
        lambda *refs: rollout_kernel(factor_scale, width, *refs),
        "rollout",
        (own, own),
        [SMEM] + [VMEM] * 5,
    )(place, parts, inverse, linear_op, pieces, offset[None, :])
    return (projection.T, reduced, mismatch)


def solution(mesh):
    slabs = mesh.shape["slab"]
    split = Mesh(mesh.devices.reshape(-1, CORES, slabs), EVERY)
    whole = P(EVERY, None)
    return jax.shard_map(
        body,
        mesh=split,
        in_specs=(whole, P(), P(), P(), P()),
        out_specs=(whole, whole, whole),
        check_vma=False,
    )
```

```python
import math

import jax
import jax.numpy as jnp
from jax import lax
from jax.experimental import pallas as pl
from jax.experimental.pallas import tpu as pltpu
from jax.sharding import Mesh
from jax.sharding import PartitionSpec as P

EVERY = ("yz", "core", "slab")
CHIPS = ("yz", "slab")
CORES = 2
RANK = 64
CHUNKS = 4
PIECES = 2
NT = (((1,), (1,)), ((), ()))
LIMIT = pltpu.CompilerParams(vmem_limit_bytes=20 * 1024 * 1024)
SMEM = pl.BlockSpec(memory_space=pltpu.SMEM)
VMEM = pl.BlockSpec(memory_space=pltpu.VMEM)
HBM = pl.BlockSpec(memory_space=pltpu.HBM)


def pieces_of(value, count, axis=0):
    pieces = []
    for _ in range(count):
        piece = value.astype(jnp.bfloat16)
        pieces.append(piece)
        value = value - piece.astype(jnp.float32)
    return jnp.concatenate(pieces, axis=axis)


def fold_rows(value, count):
    part = value.shape[0] // count
    return sum(value[i * part : (i + 1) * part] for i in range(count))


def fold_lanes(value, count):
    part = value.shape[1] // count
    return sum(value[:, i * part : (i + 1) * part] for i in range(count))


def dot_nt(left, right):
    return lax.dot_general(left, right, NT, preferred_element_type=jnp.float32)


def passes(inner, block, count, acc_ref):
    held = None
    for i in range(count):
        value = inner(i)
        if held is not None:
            part = jnp.dot(held, block(i - 1), preferred_element_type=jnp.float32)
            acc_ref[...] = part if i == 1 else acc_ref[...] + part
        held = pieces_of(value, PIECES)
    part = jnp.dot(held, block(count - 1), preferred_element_type=jnp.float32)
    return fold_rows(acc_ref[...] + part, PIECES)


def put_tiles(out_ref, value):
    wide = value.shape[1] // 128
    for i in range(out_ref.shape[0]):
        a, b = divmod(i, wide)
        out_ref[i] = value[8 * a : 8 * a + 8, 128 * b : 128 * b + 128]


def get_tiles(ref):
    tall = RANK // 8
    wide = ref.shape[0] // tall
    rows = [
        jnp.concatenate([ref[a * wide + b] for b in range(wide)], axis=1) for a in range(tall)
    ]
    return jnp.concatenate(rows, axis=0)


def power_kernel(core_ref, x_hbm, start_hbm, send_ref, x_ref, inner_ref, start_ref, acc_ref, sems):
    half = x_ref.shape[1] // CORES
    rows = x_ref.shape[0] // CHUNKS
    copies = []
    for k in range(CORES):
        source = pl.multiple_of(half * jnp.bitwise_xor(core_ref[0], k), half)
        there, here = pl.ds(source, half), pl.ds(k * half, half)
        copies.append(
            [pltpu.make_async_copy(start_hbm.at[:, there], start_ref.at[:, here], sems.at[k, CHUNKS])]
            + [
                pltpu.make_async_copy(
                    x_hbm.at[pl.ds(i * rows, rows), there],
                    x_ref.at[pl.ds(i * rows, rows), here],
                    sems.at[k, i],
                )
                for i in range(CHUNKS)
            ]
        )
    for pair in zip(*copies):
        for copy in pair:
            copy.start()
    for k in range(CORES):
        copies[k][0].wait()
    weights = pieces_of(start_ref[...], PIECES)

    def inner(i):
        for k in range(CORES):
            copies[k][i + 1].wait()
        value = fold_rows(dot_nt(weights, x_ref[pl.ds(i * rows, rows), :]), PIECES)
        inner_ref[:, pl.ds(i * rows, rows)] = pieces_of(value, PIECES)
        return value

    put_tiles(
        send_ref,
        passes(inner, lambda i: x_ref[pl.ds(i * rows, rows), half:], CHUNKS, acc_ref),
    )


def own_power_kernel(inner_ref, x_ref, keep_ref):
    half = x_ref.shape[1] // CORES
    power = jnp.dot(inner_ref[...], x_ref[:, :half], preferred_element_type=jnp.float32)
    put_tiles(keep_ref, fold_rows(power, PIECES))


def add_kernel(keep_ref, came_ref, out_ref):
    out_ref[...] = keep_ref[...] + came_ref[...]


def spread_kernel(parts_ref, out_ref):
    out_ref[...] = jnp.broadcast_to(jnp.sum(parts_ref[...], axis=0)[None], out_ref.shape)


def own_modes_kernel(x_ref, own_ref, modes_ref):
    half = x_ref.shape[1] // CORES
    weights = pieces_of(get_tiles(own_ref), PIECES)
    modes_ref[...] = fold_rows(dot_nt(weights, x_ref[:, :half]), PIECES)


def coords_kernel(core_ref, x_ref, own_modes_ref, other_ref, keep_ref, send_ref, modes_ref, acc_ref):
    half = x_ref.shape[1] // CORES
    rows = x_ref.shape[0] // CHUNKS
    weights = pieces_of(get_tiles(other_ref), PIECES)

    def inner(i):
        here = pl.ds(i * rows, rows)
        value = fold_rows(dot_nt(weights, x_ref[here, half:]), PIECES)
        value = own_modes_ref[:, here] + value
        modes_ref[:, here] = value
        return value

    coords = passes(inner, lambda i: x_ref[pl.ds(i * rows, rows), :], CHUNKS, acc_ref).T
    first = core_ref[0] == 0
    own, other = coords[:half], coords[half:]
    coords = jnp.concatenate([jnp.where(first, own, other), jnp.where(first, other, own)], axis=0)
    groups, deep, _ = keep_ref.shape
    coords = coords.reshape(groups, coords.shape[0] // groups, RANK)
    after = jnp.concatenate([coords[1:, :8], coords[:1, :8]], axis=0)
    coords = jnp.concatenate([coords, after], axis=1)
    span = deep - 8
    packed = [
        jnp.concatenate(
            [coords[:, 2 * span * c : 2 * span * c + deep], coords[:, 2 * span * c + span :][:, :deep]],
            axis=-1,
        )
        for c in range(CORES)
    ]
    keep_ref[...] = jnp.where(first, packed[0], packed[1])
    send_ref[...] = jnp.where(first, packed[1], packed[0])


def correlation_kernel(own_ref, other_ref, corr_ref):
    power = jnp.concatenate([get_tiles(own_ref), get_tiles(other_ref)], axis=1)
    pieces = pieces_of(power, 3)
    corr_ref[...] = fold_rows(fold_lanes(dot_nt(pieces, pieces), 3), 3)


def pair_kernel(keep_ref, came_ref, out_ref):
    total = keep_ref[...] + came_ref[...]
    groups = total.shape[0]
    chips, share, _ = out_ref.shape
    slabs = chips // groups
    chunks = []
    for x in range(slabs):
        side, place = divmod(x * share, total.shape[1] - 8)
        rows = total[:, place : place + share + 8, side * RANK : (side + 1) * RANK]
        chunks.append(jnp.concatenate([rows[:, :share], rows[:, 2 : share + 2]], axis=-1))
    out_ref[...] = jnp.stack(chunks, axis=1).reshape(out_ref.shape)


def spread_lane(line, k):
    return jnp.broadcast_to(line[:, k : k + 1], line.shape)


def factor_kernel(
    corr_ref, modes_hbm, quad_hbm, projection_ref, inverse_ref, pieces_ref, modes_ref, quad_ref, sems
):
    quad_fetch = pltpu.make_async_copy(quad_hbm, quad_ref, sems.at[0])
    modes_fetch = pltpu.make_async_copy(modes_hbm, modes_ref, sems.at[1])
    quad_fetch.start()
    modes_fetch.start()
    row = lax.broadcasted_iota(jnp.int32, (RANK, RANK), 0)
    column = lax.broadcasted_iota(jnp.int32, (RANK, RANK), 1)
    unit = jnp.where(row == column, jnp.float32(1.0), jnp.float32(0.0))
    work = jnp.concatenate([corr_ref[...], unit], axis=1)
    index = lax.broadcasted_iota(jnp.int32, (RANK, 1), 0)
    top = 0
    for k in range(0, RANK, 2):
        first, second = work[k - top : k - top + 1], work[k - top + 1 : k - top + 2]
        pivot, cross = spread_lane(first, k), spread_lane(first, k + 1)
        inverse = 1.0 / pivot
        ratio = cross * inverse
        other = spread_lane(second, k + 1) - cross * ratio
        second = second - ratio * first
        inverse_ref[k : k + 1] = first[:, RANK:] * (1.0 / jnp.sqrt(pivot[:, RANK:]))
        inverse_ref[k + 1 : k + 2] = second[:, RANK:] * (1.0 / jnp.sqrt(other[:, RANK:]))
        if k + 2 == RANK:
            break
        place = (k + 2) // 8 * 8
        work = work[place - top :]
        top = place
        below = index[top:] > k + 1
        left = jnp.where(below, work[:, k : k + 1], 0.0)
        right = jnp.where(below, work[:, k + 1 : k + 2], 0.0)
        scaled = second * (1.0 / other)
        work = work - (left * (first * inverse - ratio * scaled) + right * scaled)
    quad_fetch.wait()
    pieces_ref[...] = pieces_of(quad_ref[...], 3).T
    modes_fetch.wait()
    modes = jnp.dot(
        inverse_ref[...],
        modes_ref[...],
        precision=lax.Precision.HIGHEST,
        preferred_element_type=jnp.float32,
    )
    projection_ref[...] = modes.astype(jnp.bfloat16)


def rollout_kernel(
    scale, width, place_ref, parts_ref, inverse_ref, linear_ref, pieces_ref, offset_ref,
    reduced_ref, mismatch_ref,
):
    packed = jnp.sum(parts_ref[...], axis=0)
    share = packed.shape[0]
    coords = jnp.concatenate([packed[:, :RANK], packed[:, RANK:]], axis=0)
    coords = scale * lax.dot_general(
        coords,
        inverse_ref[...],
        NT,
        precision=lax.Precision.HIGHEST,
        preferred_element_type=jnp.float32,
    )
    state, target = coords[:share], coords[share:]
    reduced_ref[...] = state
    pieces = pieces_ref[...]
    upper = lax.broadcasted_iota(jnp.int32, (share, 2 * RANK), 1) >= RANK
    for _ in range(2):
        twice = jnp.concatenate([state, state], axis=1)
        pairs = jnp.concatenate(
            [
                jnp.where(upper, state[:, 2 * i + 1 : 2 * i + 2], state[:, 2 * i : 2 * i + 1])
                * twice
                for i in range(RANK // 2)
            ],
            axis=1,
        )
        quadratic = jnp.dot(pieces_of(pairs, 3), pieces, preferred_element_type=jnp.float32)
        quadratic = fold_rows(fold_lanes(quadratic, 3), 3)
        linear = jnp.dot(
            state,
            linear_ref[...],
            precision=lax.Precision.HIGHEST,
            preferred_element_type=jnp.float32,
        )
        state = state + 0.25 * (linear + quadratic + offset_ref[...])
    position = place_ref[0] * share + lax.broadcasted_iota(jnp.int32, (share, 1), 0)
    mismatch_ref[...] = jnp.where(position < width - 2, state - target, jnp.float32(0.0))


def in_hbm(value):
    return pltpu.with_memory_space_constraint(value, pltpu.HBM)


def call(kernel, name, outs, ins, scratch=()):
    return pl.pallas_call(
        kernel,
        out_shape=outs,
        in_specs=ins,
        out_specs=jax.tree.map(lambda _: VMEM, outs),
        scratch_shapes=list(scratch),
        compiler_params=LIMIT,
        name=name,
    )


def body(snapshots, start_block, linear_op, quad_op, offset):
    devices = lax.axis_size(EVERY)
    rows, width = snapshots.shape
    share = width // devices
    f32 = jnp.float32
    shape = jax.ShapeDtypeStruct
    chips = devices // CORES
    tiles = shape((chips, RANK * share // 128, 128), f32)
    small = shape((RANK, RANK), f32)
    own = shape((share, RANK), f32)
    core, place = lax.axis_index("core")[None], lax.axis_index(EVERY)[None]
    start_block, core, place = lax.optimization_barrier((start_block, core, place))
    send, held, inner = call(
        power_kernel,
        "power",
        (
            tiles,
            shape((rows, width), jnp.bfloat16),
            shape((PIECES * RANK, rows), jnp.bfloat16),
        ),
        [SMEM, HBM, HBM],
        [
            pltpu.VMEM((RANK, width), f32),
            pltpu.VMEM((PIECES * RANK, width // CORES), f32),
            pltpu.SemaphoreType.DMA((CORES, CHUNKS + 1)),
        ],
    )(core, in_hbm(snapshots), in_hbm(start_block.T))
    swap = [(0, 1), (1, 0)]
    came = lax.ppermute(send, "core", swap)
    keep = call(own_power_kernel, "own_power", tiles, [VMEM, VMEM])(inner, held)
    parts = call(add_kernel, "add", tiles, [VMEM, VMEM])(keep, came)
    parts = lax.all_to_all(parts, CHIPS, 0, 0, tiled=True)
    spread = call(spread_kernel, "spread", tiles, [VMEM])(parts)
    mine = lax.all_to_all(spread, CHIPS, 0, 0, tiled=True)
    theirs = lax.ppermute(mine, "core", swap)
    own_modes = call(own_modes_kernel, "own_modes", shape((RANK, rows), f32), [VMEM, VMEM])(
        held, mine
    )
    groups = lax.axis_size("yz")
    deep = width // groups // CORES // 2 + 8
    packed = shape((groups, deep, 2 * RANK), f32)
    keep, send, modes = call(
        coords_kernel,
        "coords",
        (packed, packed, shape((RANK, rows), f32)),
        [SMEM, VMEM, VMEM, VMEM],
        [pltpu.VMEM((PIECES * RANK, width), f32)],
    )(core, held, own_modes, theirs)
    came = lax.ppermute(send, "core", swap)
    correlation = call(correlation_kernel, "correlation", small, [VMEM, VMEM])(mine, theirs)
    came, correlation = lax.optimization_barrier((came, correlation))
    chunks = shape((chips, share, 2 * RANK), f32)
    parts = call(pair_kernel, "pair", chunks, [VMEM, VMEM])(keep, came)
    parts = lax.all_to_all(parts, CHIPS, 0, 0, tiled=True)
    projection, inverse, pieces = call(
        factor_kernel,
        "factor",
        (
            shape((RANK, rows), jnp.bfloat16),
            small,
            shape((RANK * RANK, 3 * RANK), jnp.bfloat16),
        ),
        [VMEM, HBM, HBM],
        [
            pltpu.VMEM((RANK, rows), f32),
            pltpu.VMEM((RANK, RANK * RANK), f32),
            pltpu.SemaphoreType.DMA((2,)),
        ],
    )(correlation, in_hbm(modes), in_hbm(quad_op.T))
    factor_scale = math.sqrt(width) / (rows * devices)
    reduced, mismatch = call(
        lambda *refs: rollout_kernel(factor_scale, width, *refs),
        "rollout",
        (own, own),
        [SMEM] + [VMEM] * 5,
    )(place, parts, inverse, linear_op, pieces, offset[None, :])
    return (projection.T, reduced, mismatch)


def solution(mesh):
    slabs = mesh.shape["slab"]
    split = Mesh(mesh.devices.reshape(-1, CORES, slabs), EVERY)
    whole = P(EVERY, None)
    return jax.shard_map(
        body,
        mesh=split,
        in_specs=(whole, P(), P(), P(), P()),
        out_specs=(whole, whole, whole),
        check_vma=False,
    )
```

```python
import math

import jax
import jax.numpy as jnp
from jax import lax
from jax.experimental import pallas as pl
from jax.experimental.pallas import tpu as pltpu
from jax.sharding import Mesh
from jax.sharding import PartitionSpec as P

EVERY = ("yz", "core", "slab")
CHIPS = ("yz", "slab")
CORES = 2
RANK = 64
CHUNKS = 4
PIECES = 2
NT = (((1,), (1,)), ((), ()))
LIMIT = pltpu.CompilerParams(vmem_limit_bytes=20 * 1024 * 1024)
VMEM = pl.BlockSpec(memory_space=pltpu.VMEM)
HBM = pl.BlockSpec(memory_space=pltpu.HBM)


def pieces_of(value, count, axis=0):
    pieces = []
    for _ in range(count):
        piece = value.astype(jnp.bfloat16)
        pieces.append(piece)
        value = value - piece.astype(jnp.float32)
    return jnp.concatenate(pieces, axis=axis)


def fold_rows(value, count):
    part = value.shape[0] // count
    return sum(value[i * part : (i + 1) * part] for i in range(count))


def fold_lanes(value, count):
    part = value.shape[1] // count
    return sum(value[:, i * part : (i + 1) * part] for i in range(count))


def dot_nt(left, right):
    return lax.dot_general(left, right, NT, preferred_element_type=jnp.float32)


def passes(inner, block, count, acc_ref):
    held = None
    for i in range(count):
        value = inner(i)
        if held is not None:
            part = jnp.dot(held, block(i - 1), preferred_element_type=jnp.float32)
            acc_ref[...] = part if i == 1 else acc_ref[...] + part
        held = pieces_of(value, PIECES)
    part = jnp.dot(held, block(count - 1), preferred_element_type=jnp.float32)
    return fold_rows(acc_ref[...] + part, PIECES)


def put_tiles(out_ref, value):
    wide = value.shape[1] // 128
    for i in range(out_ref.shape[0]):
        a, b = divmod(i, wide)
        out_ref[i] = value[8 * a : 8 * a + 8, 128 * b : 128 * b + 128]


def get_tiles(ref):
    tall = RANK // 8
    wide = ref.shape[0] // tall
    rows = [
        jnp.concatenate([ref[a * wide + b] for b in range(wide)], axis=1) for a in range(tall)
    ]
    return jnp.concatenate(rows, axis=0)


def power_kernel(x_hbm, start_hbm, send_ref, x_ref, inner_ref, start_ref, acc_ref, sems):
    half = x_ref.shape[1] // CORES
    rows = x_ref.shape[0] // CHUNKS
    copies = []
    for k in range(CORES):
        source = pl.multiple_of(half * jnp.bitwise_xor(lax.axis_index("core"), k), half)
        there, here = pl.ds(source, half), pl.ds(k * half, half)
        copies.append(
            [pltpu.make_async_copy(start_hbm.at[:, there], start_ref.at[:, here], sems.at[k, CHUNKS])]
            + [
                pltpu.make_async_copy(
                    x_hbm.at[pl.ds(i * rows, rows), there],
                    x_ref.at[pl.ds(i * rows, rows), here],
                    sems.at[k, i],
                )
                for i in range(CHUNKS)
            ]
        )
    for pair in zip(*copies):
        for copy in pair:
            copy.start()
    for k in range(CORES):
        copies[k][0].wait()
    weights = pieces_of(start_ref[...], PIECES)

    def inner(i):
        for k in range(CORES):
            copies[k][i + 1].wait()
        value = fold_rows(dot_nt(weights, x_ref[pl.ds(i * rows, rows), :]), PIECES)
        inner_ref[:, pl.ds(i * rows, rows)] = pieces_of(value, PIECES)
        return value

    put_tiles(
        send_ref,
        passes(inner, lambda i: x_ref[pl.ds(i * rows, rows), half:], CHUNKS, acc_ref),
    )


def own_power_kernel(inner_ref, x_ref, keep_ref):
    half = x_ref.shape[1] // CORES
    power = jnp.dot(inner_ref[...], x_ref[:, :half], preferred_element_type=jnp.float32)
    put_tiles(keep_ref, fold_rows(power, PIECES))


def add_kernel(keep_ref, came_ref, out_ref):
    out_ref[...] = keep_ref[...] + came_ref[...]


def spread_kernel(parts_ref, out_ref):
    out_ref[...] = jnp.broadcast_to(jnp.sum(parts_ref[...], axis=0)[None], out_ref.shape)


def own_modes_kernel(x_ref, own_ref, modes_ref):
    half = x_ref.shape[1] // CORES
    weights = pieces_of(get_tiles(own_ref), PIECES)
    modes = jnp.dot(x_ref[:, :half], weights.T, preferred_element_type=jnp.float32)
    modes_ref[...] = fold_rows(modes.T, PIECES)


def coords_kernel(x_ref, own_modes_ref, other_ref, keep_ref, send_ref, modes_ref, acc_ref):
    half = x_ref.shape[1] // CORES
    rows = x_ref.shape[0] // CHUNKS
    weights = pieces_of(get_tiles(other_ref), PIECES)

    def inner(i):
        here = pl.ds(i * rows, rows)
        value = fold_rows(dot_nt(weights, x_ref[here, half:]), PIECES)
        value = own_modes_ref[:, here] + value
        modes_ref[:, here] = value
        return value

    coords = passes(inner, lambda i: x_ref[pl.ds(i * rows, rows), :], CHUNKS, acc_ref)
    first = lax.axis_index("core") == 0
    own, other = coords[:, :half], coords[:, half:]
    coords = jnp.concatenate([jnp.where(first, own, other), jnp.where(first, other, own)], axis=1)
    groups, deep, _ = keep_ref.shape
    span = deep - 8
    later = jnp.concatenate([coords[:, span:], coords[:, :span]], axis=1)
    coords = jnp.concatenate([coords, later], axis=0).T.reshape(groups, -1, 2 * RANK)
    packed = [coords[:, 2 * span * c : 2 * span * c + deep] for c in range(CORES)]
    keep_ref[...] = jnp.where(first, packed[0], packed[1])
    send_ref[...] = jnp.where(first, packed[1], packed[0])


def correlation_kernel(own_ref, other_ref, corr_ref):
    power = jnp.concatenate([get_tiles(own_ref), get_tiles(other_ref)], axis=1)
    pieces = pieces_of(power, 3)
    corr_ref[...] = fold_rows(fold_lanes(dot_nt(pieces, pieces), 3), 3)


def pair_kernel(keep_ref, came_ref, out_ref):
    total = keep_ref[...] + came_ref[...]
    turned = pltpu.roll(total, RANK, axis=2)
    left = lax.broadcasted_iota(jnp.int32, (1, 1, 2 * RANK), 2) < RANK
    groups = total.shape[0]
    chips, share, _ = out_ref.shape
    slabs = chips // groups
    for x in range(slabs):
        side, place = divmod(x * share, total.shape[1] - 8)
        near, far = (total, turned) if side == 0 else (turned, total)
        chunk = jnp.where(
            left, near[:, place : place + share], far[:, place + 2 : place + share + 2]
        )
        for g in range(groups):
            out_ref[slabs * g + x] = chunk[g]


def spread_lane(line, k):
    return jnp.broadcast_to(line[:, k : k + 1], line.shape)


def factor_kernel(
    corr_ref, modes_hbm, quad_hbm, projection_ref, inverse_ref, pieces_ref, modes_ref, quad_ref, sems
):
    quad_fetch = pltpu.make_async_copy(quad_hbm, quad_ref, sems.at[0])
    modes_fetch = pltpu.make_async_copy(modes_hbm, modes_ref, sems.at[1])
    quad_fetch.start()
    modes_fetch.start()
    row = lax.broadcasted_iota(jnp.int32, (RANK, RANK), 0)
    column = lax.broadcasted_iota(jnp.int32, (RANK, RANK), 1)
    unit = jnp.where(row == column, jnp.float32(1.0), jnp.float32(0.0))
    work = jnp.concatenate([corr_ref[...], unit], axis=1)
    index = lax.broadcasted_iota(jnp.int32, (RANK, 1), 0)
    top = 0
    for k in range(0, RANK, 2):
        first, second = work[k - top : k - top + 1], work[k - top + 1 : k - top + 2]
        pivot, cross = spread_lane(first, k), spread_lane(first, k + 1)
        inverse = 1.0 / pivot
        ratio = cross * inverse
        other = spread_lane(second, k + 1) - cross * ratio
        second = second - ratio * first
        inverse_ref[k : k + 1] = first[:, RANK:] * (1.0 / jnp.sqrt(pivot[:, RANK:]))
        inverse_ref[k + 1 : k + 2] = second[:, RANK:] * (1.0 / jnp.sqrt(other[:, RANK:]))
        if k + 2 == RANK:
            break
        place = (k + 2) // 8 * 8
        work = work[place - top :]
        top = place
        below = index[top:] > k + 1
        left = jnp.where(below, work[:, k : k + 1], 0.0)
        right = jnp.where(below, work[:, k + 1 : k + 2], 0.0)
        scaled = second * (1.0 / other)
        work = work - (left * (first * inverse - ratio * scaled) + right * scaled)
    quad_fetch.wait()
    pieces_ref[...] = pieces_of(quad_ref[...], PIECES).T
    modes_fetch.wait()
    modes = jnp.dot(
        inverse_ref[...],
        modes_ref[...],
        precision=lax.Precision.HIGHEST,
        preferred_element_type=jnp.float32,
    )
    projection_ref[...] = modes.astype(jnp.bfloat16)


def rollout_kernel(
    scale, width, parts_ref, inverse_ref, linear_ref, pieces_ref, offset_ref,
    reduced_ref, mismatch_ref,
):
    packed = jnp.sum(parts_ref[...], axis=0)
    share = packed.shape[0]
    coords = jnp.concatenate([packed[:, :RANK], packed[:, RANK:]], axis=0)
    coords = scale * lax.dot_general(
        coords,
        inverse_ref[...],
        NT,
        precision=lax.Precision.HIGHEST,
        preferred_element_type=jnp.float32,
    )
    state, target = coords[:share], coords[share:]
    reduced_ref[...] = state
    pieces = pieces_ref[...]
    upper = lax.broadcasted_iota(jnp.int32, (share, 2 * RANK), 1) >= RANK
    for _ in range(2):
        twice = jnp.concatenate([state, state], axis=1)
        pairs = jnp.concatenate(
            [
                jnp.where(upper, state[:, 2 * i + 1 : 2 * i + 2], state[:, 2 * i : 2 * i + 1])
                * twice
                for i in range(RANK // 2)
            ],
            axis=1,
        )
        quadratic = jnp.dot(
            pieces_of(pairs, PIECES), pieces, preferred_element_type=jnp.float32
        )
        quadratic = fold_rows(fold_lanes(quadratic, PIECES), PIECES)
        linear = jnp.dot(
            state,
            linear_ref[...],
            precision=lax.Precision.HIGHEST,
            preferred_element_type=jnp.float32,
        )
        state = state + 0.25 * (linear + quadratic + offset_ref[...])
    position = lax.axis_index(EVERY) * share + lax.broadcasted_iota(jnp.int32, (share, 1), 0)
    mismatch_ref[...] = jnp.where(position < width - 2, state - target, jnp.float32(0.0))


def in_hbm(value):
    return pltpu.with_memory_space_constraint(value, pltpu.HBM)


def call(kernel, name, outs, ins, scratch=()):
    return pl.pallas_call(
        kernel,
        out_shape=outs,
        in_specs=ins,
        out_specs=jax.tree.map(lambda _: VMEM, outs),
        scratch_shapes=list(scratch),
        compiler_params=LIMIT,
        name=name,
    )


def body(snapshots, start_block, linear_op, quad_op, offset):
    devices = lax.axis_size(EVERY)
    rows, width = snapshots.shape
    share = width // devices
    f32 = jnp.float32
    shape = jax.ShapeDtypeStruct
    chips = devices // CORES
    tiles = shape((chips, RANK * share // 128, 128), f32)
    small = shape((RANK, RANK), f32)
    own = shape((share, RANK), f32)
    send, held, inner = call(
        power_kernel,
        "power",
        (
            tiles,
            shape((rows, width), jnp.bfloat16),
            shape((PIECES * RANK, rows), jnp.bfloat16),
        ),
        [HBM, HBM],
        [
            pltpu.VMEM((RANK, width), f32),
            pltpu.VMEM((PIECES * RANK, width // CORES), f32),
            pltpu.SemaphoreType.DMA((CORES, CHUNKS + 1)),
        ],
    )(in_hbm(snapshots), in_hbm(start_block.T))
    swap = [(0, 1), (1, 0)]
    came = lax.ppermute(send, "core", swap)
    keep = call(own_power_kernel, "own_power", tiles, [VMEM, VMEM])(inner, held)
    parts = call(add_kernel, "add", tiles, [VMEM, VMEM])(keep, came)
    parts = lax.all_to_all(parts, CHIPS, 0, 0, tiled=True)
    spread = call(spread_kernel, "spread", tiles, [VMEM])(parts)
    mine = lax.all_to_all(spread, CHIPS, 0, 0, tiled=True)
    theirs = lax.ppermute(mine, "core", swap)
    own_modes = call(own_modes_kernel, "own_modes", shape((RANK, rows), f32), [VMEM, VMEM])(
        held, mine
    )
    groups = lax.axis_size("yz")
    deep = width // groups // CORES // 2 + 8
    packed = shape((groups, deep, 2 * RANK), f32)
    keep, send, modes = call(
        coords_kernel,
        "coords",
        (packed, packed, shape((RANK, rows), f32)),
        [VMEM, VMEM, VMEM],
        [pltpu.VMEM((PIECES * RANK, width), f32)],
    )(held, own_modes, theirs)
    came = lax.ppermute(send, "core", swap)
    correlation = call(correlation_kernel, "correlation", small, [VMEM, VMEM])(mine, theirs)
    came, correlation = lax.optimization_barrier((came, correlation))
    chunks = shape((chips, share, 2 * RANK), f32)
    parts = call(pair_kernel, "pair", chunks, [VMEM, VMEM])(keep, came)
    parts = lax.all_to_all(parts, CHIPS, 0, 0, tiled=True)
    projection, inverse, pieces = call(
        factor_kernel,
        "factor",
        (
            shape((RANK, rows), jnp.bfloat16),
            small,
            shape((RANK * RANK, PIECES * RANK), jnp.bfloat16),
        ),
        [VMEM, HBM, HBM],
        [
            pltpu.VMEM((RANK, rows), f32),
            pltpu.VMEM((RANK, RANK * RANK), f32),
            pltpu.SemaphoreType.DMA((2,)),
        ],
    )(correlation, in_hbm(modes), in_hbm(quad_op.T))
    factor_scale = math.sqrt(width) / (rows * devices)
    reduced, mismatch = call(
        lambda *refs: rollout_kernel(factor_scale, width, *refs),
        "rollout",
        (own, own),
        [VMEM] * 5,
    )(parts, inverse, linear_op, pieces, offset[None, :])
    return (projection.T, reduced, mismatch)


def solution(mesh):
    slabs = mesh.shape["slab"]
    split = Mesh(mesh.devices.reshape(-1, CORES, slabs), EVERY)
    whole = P(EVERY, None)
    return jax.shard_map(
        body,
        mesh=split,
        in_specs=(whole, P(), P(), P(), P()),
        out_specs=(whole, whole, whole),
        check_vma=False,
    )
```

```python
import math

import jax
import jax.numpy as jnp
from jax import lax
from jax.experimental import pallas as pl
from jax.experimental.pallas import tpu as pltpu
from jax.sharding import Mesh
from jax.sharding import PartitionSpec as P

EVERY = ("yz", "core", "slab")
CHIPS = ("yz", "slab")
CORES = 2
RANK = 64
CHUNKS = 4
BLOCKS = 2
PIECES = 2
NT = (((1,), (1,)), ((), ()))
LIMIT = pltpu.CompilerParams(vmem_limit_bytes=20 * 1024 * 1024)
VMEM = pl.BlockSpec(memory_space=pltpu.VMEM)
HBM = pl.BlockSpec(memory_space=pltpu.HBM)


def pieces_of(value, count, axis=0):
    pieces = []
    for _ in range(count):
        piece = value.astype(jnp.bfloat16)
        pieces.append(piece)
        value = value - piece.astype(jnp.float32)
    return jnp.concatenate(pieces, axis=axis)


def fold_rows(value, count):
    part = value.shape[0] // count
    return sum(value[i * part : (i + 1) * part] for i in range(count))


def fold_lanes(value, count):
    part = value.shape[1] // count
    return sum(value[:, i * part : (i + 1) * part] for i in range(count))


def dot_nt(left, right):
    return lax.dot_general(left, right, NT, preferred_element_type=jnp.float32)


def passes(inner, block, count, acc_ref):
    held = None
    for i in range(count):
        value = inner(i)
        if held is not None:
            part = jnp.dot(held, block(i - 1), preferred_element_type=jnp.float32)
            acc_ref[...] = part if i == 1 else acc_ref[...] + part
        held = pieces_of(value, PIECES)
    part = jnp.dot(held, block(count - 1), preferred_element_type=jnp.float32)
    return fold_rows(acc_ref[...] + part, PIECES)


def put_tiles(out_ref, value):
    wide = value.shape[1] // 128
    for i in range(out_ref.shape[0]):
        a, b = divmod(i, wide)
        out_ref[i] = value[8 * a : 8 * a + 8, 128 * b : 128 * b + 128]


def get_tiles(ref):
    tall = RANK // 8
    wide = ref.shape[0] // tall
    rows = [
        jnp.concatenate([ref[a * wide + b] for b in range(wide)], axis=1) for a in range(tall)
    ]
    return jnp.concatenate(rows, axis=0)


def power_kernel(x_hbm, start_hbm, send_ref, x_ref, inner_ref, start_ref, acc_ref, sems):
    half = x_ref.shape[1] // CORES
    rows = x_ref.shape[0] // CHUNKS
    copies = []
    for k in range(CORES):
        source = pl.multiple_of(half * jnp.bitwise_xor(lax.axis_index("core"), k), half)
        there, here = pl.ds(source, half), pl.ds(k * half, half)
        copies.append(
            [pltpu.make_async_copy(start_hbm.at[:, there], start_ref.at[:, here], sems.at[k, CHUNKS])]
            + [
                pltpu.make_async_copy(
                    x_hbm.at[pl.ds(i * rows, rows), there],
                    x_ref.at[pl.ds(i * rows, rows), here],
                    sems.at[k, i],
                )
                for i in range(CHUNKS)
            ]
        )
    for pair in zip(*copies):
        for copy in pair:
            copy.start()
    for k in range(CORES):
        copies[k][0].wait()
    weights = pieces_of(start_ref[...], PIECES)

    def inner(i):
        for k in range(CORES):
            copies[k][i + 1].wait()
        value = fold_rows(dot_nt(weights, x_ref[pl.ds(i * rows, rows), :]), PIECES)
        inner_ref[:, pl.ds(i * rows, rows)] = pieces_of(value, PIECES)
        return value

    put_tiles(
        send_ref,
        passes(inner, lambda i: x_ref[pl.ds(i * rows, rows), half:], CHUNKS, acc_ref),
    )


def own_power_kernel(inner_ref, x_ref, keep_ref):
    half = x_ref.shape[1] // CORES
    power = jnp.dot(inner_ref[...], x_ref[:, :half], preferred_element_type=jnp.float32)
    put_tiles(keep_ref, fold_rows(power, PIECES))


def add_kernel(keep_ref, came_ref, out_ref):
    out_ref[...] = keep_ref[...] + came_ref[...]


def spread_kernel(parts_ref, out_ref):
    out_ref[...] = jnp.broadcast_to(jnp.sum(parts_ref[...], axis=0)[None], out_ref.shape)


def own_modes_kernel(x_ref, own_ref, modes_ref):
    half = x_ref.shape[1] // CORES
    weights = pieces_of(get_tiles(own_ref), PIECES)
    modes = jnp.dot(x_ref[:, :half], weights.T, preferred_element_type=jnp.float32)
    modes_ref[...] = fold_rows(modes.T, PIECES)


def coords_kernel(x_ref, own_modes_ref, other_ref, keep_ref, send_ref, modes_ref, acc_ref):
    half = x_ref.shape[1] // CORES
    rows = x_ref.shape[0] // BLOCKS
    weights = pieces_of(get_tiles(other_ref), PIECES).T

    def inner(i):
        here = pl.ds(i * rows, rows)
        value = jnp.dot(x_ref[here, half:], weights, preferred_element_type=jnp.float32)
        value = fold_rows(value.T, PIECES)
        value = own_modes_ref[:, here] + value
        modes_ref[:, here] = value
        return value

    coords = passes(inner, lambda i: x_ref[pl.ds(i * rows, rows), :], BLOCKS, acc_ref)
    first = lax.axis_index("core") == 0
    own, other = coords[:, :half], coords[:, half:]
    coords = jnp.concatenate([jnp.where(first, own, other), jnp.where(first, other, own)], axis=1)
    groups, deep, _ = keep_ref.shape
    span = deep - 8
    later = jnp.concatenate([coords[:, span:], coords[:, :span]], axis=1)
    coords = jnp.concatenate([coords, later], axis=0).T.reshape(groups, -1, 2 * RANK)
    packed = [coords[:, 2 * span * c : 2 * span * c + deep] for c in range(CORES)]
    keep_ref[...] = jnp.where(first, packed[0], packed[1])
    send_ref[...] = jnp.where(first, packed[1], packed[0])


def correlation_kernel(own_ref, other_ref, corr_ref):
    power = jnp.concatenate([get_tiles(own_ref), get_tiles(other_ref)], axis=1)
    pieces = pieces_of(power, 3)
    corr_ref[...] = fold_rows(fold_lanes(dot_nt(pieces, pieces), 3), 3)


def pair_kernel(keep_ref, came_ref, out_ref):
    total = keep_ref[...] + came_ref[...]
    turned = pltpu.roll(total, RANK, axis=2)
    left = lax.broadcasted_iota(jnp.int32, (1, 1, 2 * RANK), 2) < RANK
    groups = total.shape[0]
    chips, pairs = out_ref.shape[:2]
    slabs = chips // groups
    share = 4 * pairs - 4
    for x in range(slabs):
        side, place = divmod(x * share, total.shape[1] - 8)
        near, far = (total, turned) if side == 0 else (turned, total)
        middle = place + share // 2
        chunk = jnp.where(
            left, near[:, place : place + 2 * pairs], far[:, middle : middle + 2 * pairs]
        )
        for g in range(groups):
            for i in range(pairs):
                out_ref[slabs * g + x, i] = chunk[g, 2 * i : 2 * i + 2]


def spread_lane(line, k):
    return jnp.broadcast_to(line[:, k : k + 1], line.shape)


def factor_kernel(
    corr_ref, modes_hbm, quad_hbm, projection_ref, inverse_ref, pieces_ref, modes_ref, quad_ref, sems
):
    quad_fetch = pltpu.make_async_copy(quad_hbm, quad_ref, sems.at[0])
    modes_fetch = pltpu.make_async_copy(modes_hbm, modes_ref, sems.at[1])
    quad_fetch.start()
    modes_fetch.start()
    row = lax.broadcasted_iota(jnp.int32, (RANK, RANK), 0)
    column = lax.broadcasted_iota(jnp.int32, (RANK, RANK), 1)
    unit = jnp.where(row == column, jnp.float32(1.0), jnp.float32(0.0))
    work = jnp.concatenate([corr_ref[...], unit], axis=1)
    index = lax.broadcasted_iota(jnp.int32, (RANK, 1), 0)
    top = 0
    for k in range(0, RANK, 2):
        first, second = work[k - top : k - top + 1], work[k - top + 1 : k - top + 2]
        pivot, cross = spread_lane(first, k), spread_lane(first, k + 1)
        inverse = 1.0 / pivot
        ratio = cross * inverse
        other = spread_lane(second, k + 1) - cross * ratio
        second = second - ratio * first
        inverse_ref[k : k + 1] = first[:, RANK:] * (1.0 / jnp.sqrt(pivot[:, RANK:]))
        inverse_ref[k + 1 : k + 2] = second[:, RANK:] * (1.0 / jnp.sqrt(other[:, RANK:]))
        if k + 2 == RANK:
            break
        place = (k + 2) // 8 * 8
        work = work[place - top :]
        top = place
        below = index[top:] > k + 1
        left = jnp.where(below, work[:, k : k + 1], 0.0)
        right = jnp.where(below, work[:, k + 1 : k + 2], 0.0)
        scaled = second * (1.0 / other)
        work = work - (left * (first * inverse - ratio * scaled) + right * scaled)
    quad_fetch.wait()
    pieces_ref[...] = pieces_of(quad_ref[...], PIECES).T
    modes_fetch.wait()
    modes = jnp.dot(
        inverse_ref[...],
        modes_ref[...],
        precision=lax.Precision.HIGHEST,
        preferred_element_type=jnp.float32,
    )
    projection_ref[...] = modes.astype(jnp.bfloat16)


def rollout_kernel(
    scale, width, parts_ref, inverse_ref, linear_ref, pieces_ref, offset_ref,
    reduced_ref, mismatch_ref,
):
    packed = jnp.sum(parts_ref[...], axis=0)
    packed = jnp.concatenate([packed[i] for i in range(packed.shape[0])], axis=0)
    sides = packed[:, :RANK], packed[:, RANK:]
    share = reduced_ref.shape[0]
    half = share // 2
    coords = jnp.concatenate(
        [side[:half] for side in sides] + [side[2 : half + 2] for side in sides], axis=0
    )
    coords = scale * lax.dot_general(
        coords,
        inverse_ref[...],
        NT,
        precision=lax.Precision.HIGHEST,
        preferred_element_type=jnp.float32,
    )
    state, target = coords[:share], coords[share:]
    reduced_ref[...] = state
    pieces = pieces_ref[...]
    upper = lax.broadcasted_iota(jnp.int32, (share, 2 * RANK), 1) >= RANK
    for _ in range(2):
        twice = jnp.concatenate([state, state], axis=1)
        pairs = jnp.concatenate(
            [
                jnp.where(upper, state[:, 2 * i + 1 : 2 * i + 2], state[:, 2 * i : 2 * i + 1])
                * twice
                for i in range(RANK // 2)
            ],
            axis=1,
        )
        quadratic = jnp.dot(
            pieces_of(pairs, PIECES), pieces, preferred_element_type=jnp.float32
        )
        quadratic = fold_rows(fold_lanes(quadratic, PIECES), PIECES)
        linear = jnp.dot(
            state,
            linear_ref[...],
            precision=lax.Precision.HIGHEST,
            preferred_element_type=jnp.float32,
        )
        state = state + 0.25 * (linear + quadratic + offset_ref[...])
    position = lax.axis_index(EVERY) * share + lax.broadcasted_iota(jnp.int32, (share, 1), 0)
    mismatch_ref[...] = jnp.where(position < width - 2, state - target, jnp.float32(0.0))


def in_hbm(value):
    return pltpu.with_memory_space_constraint(value, pltpu.HBM)


def call(kernel, name, outs, ins, scratch=()):
    return pl.pallas_call(
        kernel,
        out_shape=outs,
        in_specs=ins,
        out_specs=jax.tree.map(lambda _: VMEM, outs),
        scratch_shapes=list(scratch),
        compiler_params=LIMIT,
        name=name,
    )


def body(snapshots, start_block, linear_op, quad_op, offset):
    devices = lax.axis_size(EVERY)
    rows, width = snapshots.shape
    share = width // devices
    f32 = jnp.float32
    shape = jax.ShapeDtypeStruct
    chips = devices // CORES
    tiles = shape((chips, RANK * share // 128, 128), f32)
    small = shape((RANK, RANK), f32)
    own = shape((share, RANK), f32)
    send, held, inner = call(
        power_kernel,
        "power",
        (
            tiles,
            shape((rows, width), jnp.bfloat16),
            shape((PIECES * RANK, rows), jnp.bfloat16),
        ),
        [HBM, HBM],
        [
            pltpu.VMEM((RANK, width), f32),
            pltpu.VMEM((PIECES * RANK, width // CORES), f32),
            pltpu.SemaphoreType.DMA((CORES, CHUNKS + 1)),
        ],
    )(in_hbm(snapshots), in_hbm(start_block.T))
    swap = [(0, 1), (1, 0)]
    came = lax.ppermute(send, "core", swap)
    keep = call(own_power_kernel, "own_power", tiles, [VMEM, VMEM])(inner, held)
    parts = call(add_kernel, "add", tiles, [VMEM, VMEM])(keep, came)
    parts = lax.all_to_all(parts, CHIPS, 0, 0, tiled=True)
    spread = call(spread_kernel, "spread", tiles, [VMEM])(parts)
    mine = lax.all_to_all(spread, CHIPS, 0, 0, tiled=True)
    theirs = lax.ppermute(mine, "core", swap)
    own_modes = call(own_modes_kernel, "own_modes", shape((RANK, rows), f32), [VMEM, VMEM])(
        held, mine
    )
    groups = lax.axis_size("yz")
    deep = width // groups // CORES // 2 + 8
    packed = shape((groups, deep, 2 * RANK), f32)
    keep, send, modes = call(
        coords_kernel,
        "coords",
        (packed, packed, shape((RANK, rows), f32)),
        [VMEM, VMEM, VMEM],
        [pltpu.VMEM((PIECES * RANK, width), f32)],
    )(held, own_modes, theirs)
    came = lax.ppermute(send, "core", swap)
    correlation = call(correlation_kernel, "correlation", small, [VMEM, VMEM])(mine, theirs)
    came, correlation = lax.optimization_barrier((came, correlation))
    chunks = shape((chips, share // 4 + 1, 2, 2 * RANK), f32)
    parts = call(pair_kernel, "pair", chunks, [VMEM, VMEM])(keep, came)
    parts = lax.all_to_all(parts, CHIPS, 0, 0, tiled=True)
    projection, inverse, pieces = call(
        factor_kernel,
        "factor",
        (
            shape((RANK, rows), jnp.bfloat16),
            small,
            shape((RANK * RANK, PIECES * RANK), jnp.bfloat16),
        ),
        [VMEM, HBM, HBM],
        [
            pltpu.VMEM((RANK, rows), f32),
            pltpu.VMEM((RANK, RANK * RANK), f32),
            pltpu.SemaphoreType.DMA((2,)),
        ],
    )(correlation, in_hbm(modes), in_hbm(quad_op.T))
    factor_scale = math.sqrt(width) / (rows * devices)
    reduced, mismatch = call(
        lambda *refs: rollout_kernel(factor_scale, width, *refs),
        "rollout",
        (own, own),
        [VMEM] * 5,
    )(parts, inverse, linear_op, pieces, offset[None, :])
    return (projection.T, reduced, mismatch)


def solution(mesh):
    slabs = mesh.shape["slab"]
    split = Mesh(mesh.devices.reshape(-1, CORES, slabs), EVERY)
    whole = P(EVERY, None)
    return jax.shard_map(
        body,
        mesh=split,
        in_specs=(whole, P(), P(), P(), P()),
        out_specs=(whole, whole, whole),
        check_vma=False,
    )
```

```python
import math

import jax
import jax.numpy as jnp
from jax import lax
from jax.experimental import pallas as pl
from jax.experimental.pallas import tpu as pltpu
from jax.sharding import Mesh
from jax.sharding import PartitionSpec as P

EVERY = ("yz", "core", "slab")
CHIPS = ("yz", "slab")
CORES = 2
RANK = 64
CHUNKS = 4
BLOCKS = 2
PIECES = 2
NT = (((1,), (1,)), ((), ()))
LIMIT = pltpu.CompilerParams(vmem_limit_bytes=20 * 1024 * 1024)
VMEM = pl.BlockSpec(memory_space=pltpu.VMEM)
HBM = pl.BlockSpec(memory_space=pltpu.HBM)


def pieces_of(value, count, axis=0):
    pieces = []
    for _ in range(count):
        piece = value.astype(jnp.bfloat16)
        pieces.append(piece)
        value = value - piece.astype(jnp.float32)
    return jnp.concatenate(pieces, axis=axis)


def fold_rows(value, count):
    part = value.shape[0] // count
    return sum(value[i * part : (i + 1) * part] for i in range(count))


def fold_lanes(value, count):
    part = value.shape[1] // count
    return sum(value[:, i * part : (i + 1) * part] for i in range(count))


def dot_nt(left, right):
    return lax.dot_general(left, right, NT, preferred_element_type=jnp.float32)


def passes(inner, block, count, acc_ref):
    held = None
    for i in range(count):
        value = inner(i)
        if held is not None:
            part = jnp.dot(held, block(i - 1), preferred_element_type=jnp.float32)
            acc_ref[...] = part if i == 1 else acc_ref[...] + part
        held = pieces_of(value, PIECES)
    part = jnp.dot(held, block(count - 1), preferred_element_type=jnp.float32)
    return fold_rows(acc_ref[...] + part, PIECES)


def put_tiles(out_ref, value):
    wide = value.shape[1] // 128
    for i in range(out_ref.shape[0]):
        a, b = divmod(i, wide)
        out_ref[i] = value[8 * a : 8 * a + 8, 128 * b : 128 * b + 128]


def get_tiles(ref):
    tall = RANK // 8
    wide = ref.shape[0] // tall
    rows = [
        jnp.concatenate([ref[a * wide + b] for b in range(wide)], axis=1) for a in range(tall)
    ]
    return jnp.concatenate(rows, axis=0)


def power_kernel(x_hbm, start_hbm, send_ref, x_ref, inner_ref, start_ref, acc_ref, sems):
    half = x_ref.shape[1] // CORES
    rows = x_ref.shape[0] // CHUNKS
    copies = []
    for k in range(CORES):
        source = pl.multiple_of(half * jnp.bitwise_xor(lax.axis_index("core"), k), half)
        there, here = pl.ds(source, half), pl.ds(k * half, half)
        copies.append(
            [pltpu.make_async_copy(start_hbm.at[:, there], start_ref.at[:, here], sems.at[k, CHUNKS])]
            + [
                pltpu.make_async_copy(
                    x_hbm.at[pl.ds(i * rows, rows), there],
                    x_ref.at[pl.ds(i * rows, rows), here],
                    sems.at[k, i],
                )
                for i in range(CHUNKS)
            ]
        )
    for pair in zip(*copies):
        for copy in pair:
            copy.start()
    for k in range(CORES):
        copies[k][0].wait()
    weights = pieces_of(start_ref[...], PIECES)

    def inner(i):
        for k in range(CORES):
            copies[k][i + 1].wait()
        value = fold_rows(dot_nt(weights, x_ref[pl.ds(i * rows, rows), :]), PIECES)
        inner_ref[:, pl.ds(i * rows, rows)] = pieces_of(value, PIECES)
        return value

    put_tiles(
        send_ref,
        passes(inner, lambda i: x_ref[pl.ds(i * rows, rows), half:], CHUNKS, acc_ref),
    )


def own_power_kernel(inner_ref, x_ref, keep_ref):
    half = x_ref.shape[1] // CORES
    power = jnp.dot(inner_ref[...], x_ref[:, :half], preferred_element_type=jnp.float32)
    put_tiles(keep_ref, fold_rows(power, PIECES))


def add_kernel(keep_ref, came_ref, out_ref):
    out_ref[...] = keep_ref[...] + came_ref[...]


def spread_kernel(parts_ref, out_ref):
    out_ref[...] = jnp.broadcast_to(jnp.sum(parts_ref[...], axis=0)[None], out_ref.shape)


def own_modes_kernel(x_ref, own_ref, modes_ref):
    half = x_ref.shape[1] // CORES
    weights = pieces_of(get_tiles(own_ref), PIECES)
    modes = jnp.dot(x_ref[:, :half], weights.T, preferred_element_type=jnp.float32)
    modes_ref[...] = fold_rows(modes.T, PIECES)


def coords_kernel(x_ref, own_modes_ref, other_ref, keep_ref, send_ref, modes_ref, acc_ref):
    half = x_ref.shape[1] // CORES
    rows = x_ref.shape[0] // BLOCKS
    weights = pieces_of(get_tiles(other_ref), PIECES).T

    def inner(i):
        here = pl.ds(i * rows, rows)
        value = jnp.dot(x_ref[here, half:], weights, preferred_element_type=jnp.float32)
        value = fold_rows(value.T, PIECES)
        value = own_modes_ref[:, here] + value
        modes_ref[:, here] = value
        return value

    coords = passes(inner, lambda i: x_ref[pl.ds(i * rows, rows), :], BLOCKS, acc_ref)
    first = lax.axis_index("core") == 0
    own, other = coords[:, :half], coords[:, half:]
    coords = jnp.concatenate([jnp.where(first, own, other), jnp.where(first, other, own)], axis=1)
    groups, deep, _ = keep_ref.shape
    span = deep - 8
    later = jnp.concatenate([coords[:, span:], coords[:, :span]], axis=1)
    coords = jnp.concatenate([coords, later], axis=0).T.reshape(groups, -1, 2 * RANK)
    packed = [coords[:, 2 * span * c : 2 * span * c + deep] for c in range(CORES)]
    keep_ref[...] = jnp.where(first, packed[0], packed[1])
    send_ref[...] = jnp.where(first, packed[1], packed[0])


def correlation_kernel(own_ref, other_ref, corr_ref):
    power = jnp.concatenate([get_tiles(own_ref), get_tiles(other_ref)], axis=1)
    pieces = pieces_of(power, 3)
    corr_ref[...] = fold_rows(fold_lanes(dot_nt(pieces, pieces), 3), 3)


def pair_kernel(keep_ref, came_ref, out_hbm, out_ref, sem):
    total = keep_ref[...] + came_ref[...]
    turned = pltpu.roll(total, RANK, axis=2)
    left = lax.broadcasted_iota(jnp.int32, (1, 1, 2 * RANK), 2) < RANK
    groups = total.shape[0]
    chips, deep = out_ref.shape[:2]
    slabs = chips // groups
    share = 2 * deep - 2
    for x in range(slabs):
        side, place = divmod(x * share, total.shape[1] - 8)
        near, far = (total, turned) if side == 0 else (turned, total)
        middle = place + deep
        chunk = jnp.where(left, near[:, place:middle], far[:, middle : middle + deep])
        for g in range(groups):
            for i in range(deep):
                out_ref[slabs * g + x, i] = chunk[g, i : i + 1]
    copy = pltpu.make_async_copy(out_ref, out_hbm, sem)
    copy.start()
    copy.wait()


def spread_lane(line, k):
    return jnp.broadcast_to(line[:, k : k + 1], line.shape)


def factor_kernel(
    corr_ref, modes_hbm, quad_hbm, projection_hbm, inverse_ref, pieces_ref,
    modes_ref, quad_ref, projection_ref, sems,
):
    quad_fetch = pltpu.make_async_copy(quad_hbm, quad_ref, sems.at[0])
    modes_fetch = pltpu.make_async_copy(modes_hbm, modes_ref, sems.at[1])
    quad_fetch.start()
    modes_fetch.start()
    row = lax.broadcasted_iota(jnp.int32, (RANK, RANK), 0)
    column = lax.broadcasted_iota(jnp.int32, (RANK, RANK), 1)
    unit = jnp.where(row == column, jnp.float32(1.0), jnp.float32(0.0))
    work = jnp.concatenate([corr_ref[...], unit], axis=1)
    index = lax.broadcasted_iota(jnp.int32, (RANK, 1), 0)
    top = 0
    for k in range(0, RANK, 2):
        first, second = work[k - top : k - top + 1], work[k - top + 1 : k - top + 2]
        pivot, cross = spread_lane(first, k), spread_lane(first, k + 1)
        inverse = 1.0 / pivot
        ratio = cross * inverse
        other = spread_lane(second, k + 1) - cross * ratio
        second = second - ratio * first
        inverse_ref[k : k + 1] = first[:, RANK:] * (1.0 / jnp.sqrt(pivot[:, RANK:]))
        inverse_ref[k + 1 : k + 2] = second[:, RANK:] * (1.0 / jnp.sqrt(other[:, RANK:]))
        if k + 2 == RANK:
            break
        place = (k + 2) // 8 * 8
        work = work[place - top :]
        top = place
        below = index[top:] > k + 1
        left = jnp.where(below, work[:, k : k + 1], 0.0)
        right = jnp.where(below, work[:, k + 1 : k + 2], 0.0)
        scaled = second * (1.0 / other)
        work = work - (left * (first * inverse - ratio * scaled) + right * scaled)
    quad_fetch.wait()
    pieces_ref[...] = pieces_of(quad_ref[...], PIECES).T
    modes_fetch.wait()
    left = pieces_of(inverse_ref[...], 3)
    modes = jnp.dot(
        jnp.concatenate([left] * 3, axis=1),
        pieces_of(modes_ref[...], 3),
        preferred_element_type=jnp.float32,
    )
    projection_ref[...] = fold_rows(modes, 3).astype(jnp.bfloat16)
    copy = pltpu.make_async_copy(projection_ref, projection_hbm, sems.at[2])
    copy.start()
    copy.wait()


def rollout_kernel(
    scale, width, parts_ref, inverse_ref, linear_ref, pieces_ref, offset_ref,
    reduced_hbm, mismatch_hbm, reduced_ref, mismatch_ref, sems,
):
    packed = jnp.sum(parts_ref[...], axis=0)
    packed = jnp.concatenate([packed[i] for i in range(packed.shape[0])], axis=0)
    share = reduced_ref.shape[0]
    coords = jnp.concatenate([packed[:, :RANK], packed[:, RANK:]], axis=0)
    coords = scale * lax.dot_general(
        coords,
        inverse_ref[...],
        NT,
        precision=lax.Precision.HIGHEST,
        preferred_element_type=jnp.float32,
    )
    state, target = coords[:share], coords[2:]
    reduced_ref[...] = state
    reduced_copy = pltpu.make_async_copy(reduced_ref, reduced_hbm, sems.at[0])
    reduced_copy.start()
    pieces = pieces_ref[...]
    upper = lax.broadcasted_iota(jnp.int32, (share, 2 * RANK), 1) >= RANK
    for _ in range(2):
        twice = jnp.concatenate([state, state], axis=1)
        pairs = jnp.concatenate(
            [
                jnp.where(upper, state[:, 2 * i + 1 : 2 * i + 2], state[:, 2 * i : 2 * i + 1])
                * twice
                for i in range(RANK // 2)
            ],
            axis=1,
        )
        quadratic = jnp.dot(
            pieces_of(pairs, PIECES), pieces, preferred_element_type=jnp.float32
        )
        quadratic = fold_rows(fold_lanes(quadratic, PIECES), PIECES)
        linear = jnp.dot(
            state,
            linear_ref[...],
            precision=lax.Precision.HIGHEST,
            preferred_element_type=jnp.float32,
        )
        state = state + 0.25 * (linear + quadratic + offset_ref[...])
    position = lax.axis_index(EVERY) * share + lax.broadcasted_iota(jnp.int32, (share, 1), 0)
    mismatch_ref[...] = jnp.where(position < width - 2, state - target, jnp.float32(0.0))
    mismatch_copy = pltpu.make_async_copy(mismatch_ref, mismatch_hbm, sems.at[1])
    mismatch_copy.start()
    reduced_copy.wait()
    mismatch_copy.wait()


def in_hbm(value):
    return pltpu.with_memory_space_constraint(value, pltpu.HBM)


def call(kernel, name, outs, ins, scratch=(), places=None):
    return pl.pallas_call(
        kernel,
        out_shape=outs,
        in_specs=ins,
        out_specs=places or jax.tree.map(lambda _: VMEM, outs),
        scratch_shapes=list(scratch),
        compiler_params=LIMIT,
        name=name,
    )


def body(snapshots, start_block, linear_op, quad_op, offset):
    devices = lax.axis_size(EVERY)
    rows, width = snapshots.shape
    share = width // devices
    f32 = jnp.float32
    shape = jax.ShapeDtypeStruct
    chips = devices // CORES
    tiles = shape((chips, RANK * share // 128, 128), f32)
    small = shape((RANK, RANK), f32)
    own = shape((share, RANK), f32)
    send, held, inner = call(
        power_kernel,
        "power",
        (
            tiles,
            shape((rows, width), jnp.bfloat16),
            shape((PIECES * RANK, rows), jnp.bfloat16),
        ),
        [HBM, HBM],
        [
            pltpu.VMEM((RANK, width), f32),
            pltpu.VMEM((PIECES * RANK, width // CORES), f32),
            pltpu.SemaphoreType.DMA((CORES, CHUNKS + 1)),
        ],
    )(in_hbm(snapshots), in_hbm(start_block.T))
    swap = [(0, 1), (1, 0)]
    came = lax.ppermute(send, "core", swap)
    keep = call(own_power_kernel, "own_power", tiles, [VMEM, VMEM])(inner, held)
    parts = call(add_kernel, "add", tiles, [VMEM, VMEM])(keep, came)
    parts = lax.all_to_all(parts, CHIPS, 0, 0, tiled=True)
    spread = call(spread_kernel, "spread", tiles, [VMEM])(parts)
    mine = lax.all_to_all(spread, CHIPS, 0, 0, tiled=True)
    theirs = lax.ppermute(mine, "core", swap)
    own_modes = call(own_modes_kernel, "own_modes", shape((RANK, rows), f32), [VMEM, VMEM])(
        held, mine
    )
    groups = lax.axis_size("yz")
    deep = width // groups // CORES // 2 + 8
    packed = shape((groups, deep, 2 * RANK), f32)
    keep, send, modes = call(
        coords_kernel,
        "coords",
        (packed, packed, shape((RANK, rows), f32)),
        [VMEM, VMEM, VMEM],
        [pltpu.VMEM((PIECES * RANK, width), f32)],
    )(held, own_modes, theirs)
    came = lax.ppermute(send, "core", swap)
    correlation = call(correlation_kernel, "correlation", small, [VMEM, VMEM])(mine, theirs)
    came, correlation = lax.optimization_barrier((came, correlation))
    chunk = (chips, share // 2 + 1, 1, 2 * RANK)
    parts = call(
        pair_kernel,
        "pair",
        shape(chunk, f32),
        [VMEM, VMEM],
        [pltpu.VMEM(chunk, f32), pltpu.SemaphoreType.DMA(())],
        HBM,
    )(keep, came)
    parts = lax.all_to_all(parts, CHIPS, 0, 0, tiled=True)
    projection, inverse, pieces = call(
        factor_kernel,
        "factor",
        (
            shape((RANK, rows), jnp.bfloat16),
            small,
            shape((RANK * RANK, PIECES * RANK), jnp.bfloat16),
        ),
        [VMEM, HBM, HBM],
        [
            pltpu.VMEM((RANK, rows), f32),
            pltpu.VMEM((RANK, RANK * RANK), f32),
            pltpu.VMEM((RANK, rows), jnp.bfloat16),
            pltpu.SemaphoreType.DMA((3,)),
        ],
        (HBM, VMEM, VMEM),
    )(correlation, in_hbm(modes), in_hbm(quad_op.T))
    factor_scale = math.sqrt(width) / (rows * devices)
    reduced, mismatch = call(
        lambda *refs: rollout_kernel(factor_scale, width, *refs),
        "rollout",
        (own, own),
        [VMEM] * 5,
        [
            pltpu.VMEM((share, RANK), f32),
            pltpu.VMEM((share, RANK), f32),
            pltpu.SemaphoreType.DMA((2,)),
        ],
        (HBM, HBM),
    )(parts, inverse, linear_op, pieces, offset[None, :])
    return (projection.T, reduced, mismatch)


def solution(mesh):
    slabs = mesh.shape["slab"]
    split = Mesh(mesh.devices.reshape(-1, CORES, slabs), EVERY)
    whole = P(EVERY, None)
    return jax.shard_map(
        body,
        mesh=split,
        in_specs=(whole, P(), P(), P(), P()),
        out_specs=(whole, whole, whole),
        check_vma=False,
    )
```

```python
import math

import jax
import jax.numpy as jnp
from jax import lax
from jax.experimental import pallas as pl
from jax.experimental.pallas import tpu as pltpu
from jax.sharding import Mesh
from jax.sharding import PartitionSpec as P

EVERY = ("yz", "core", "slab")
CHIPS = ("yz", "slab")
CORES = 2
RANK = 64
CHUNKS = 4
BLOCKS = 2
PIECES = 2
NT = (((1,), (1,)), ((), ()))
LIMIT = pltpu.CompilerParams(vmem_limit_bytes=20 * 1024 * 1024)
VMEM = pl.BlockSpec(memory_space=pltpu.VMEM)
HBM = pl.BlockSpec(memory_space=pltpu.HBM)


def pieces_of(value, count, axis=0):
    pieces = []
    for _ in range(count):
        piece = value.astype(jnp.bfloat16)
        pieces.append(piece)
        value = value - piece.astype(jnp.float32)
    return jnp.concatenate(pieces, axis=axis)


def fold_rows(value, count):
    part = value.shape[0] // count
    return sum(value[i * part : (i + 1) * part] for i in range(count))


def fold_lanes(value, count):
    part = value.shape[1] // count
    return sum(value[:, i * part : (i + 1) * part] for i in range(count))


def dot_nt(left, right):
    return lax.dot_general(left, right, NT, preferred_element_type=jnp.float32)


def passes(inner, block, count, acc_ref):
    held = None
    for i in range(count):
        value = inner(i)
        if held is not None:
            part = jnp.dot(held, block(i - 1), preferred_element_type=jnp.float32)
            acc_ref[...] = part if i == 1 else acc_ref[...] + part
        held = pieces_of(value, PIECES)
    part = jnp.dot(held, block(count - 1), preferred_element_type=jnp.float32)
    return fold_rows(acc_ref[...] + part, PIECES)


def put_tiles(out_ref, value):
    wide = value.shape[1] // 128
    for i in range(out_ref.shape[0]):
        a, b = divmod(i, wide)
        out_ref[i] = value[8 * a : 8 * a + 8, 128 * b : 128 * b + 128]


def get_tiles(ref):
    tall = RANK // 8
    wide = ref.shape[0] // tall
    rows = [
        jnp.concatenate([ref[a * wide + b] for b in range(wide)], axis=1) for a in range(tall)
    ]
    return jnp.concatenate(rows, axis=0)


def power_kernel(x_hbm, start_hbm, send_ref, x_ref, inner_ref, start_ref, acc_ref, sems):
    half = x_ref.shape[1] // CORES
    rows = x_ref.shape[0] // CHUNKS
    copies = []
    for k in range(CORES):
        source = pl.multiple_of(half * jnp.bitwise_xor(lax.axis_index("core"), k), half)
        there, here = pl.ds(source, half), pl.ds(k * half, half)
        copies.append(
            [pltpu.make_async_copy(start_hbm.at[:, there], start_ref.at[:, here], sems.at[k, CHUNKS])]
            + [
                pltpu.make_async_copy(
                    x_hbm.at[pl.ds(i * rows, rows), there],
                    x_ref.at[pl.ds(i * rows, rows), here],
                    sems.at[k, i],
                )
                for i in range(CHUNKS)
            ]
        )
    for pair in zip(*copies):
        for copy in pair:
            copy.start()
    for k in range(CORES):
        copies[k][0].wait()
    weights = pieces_of(start_ref[...], PIECES)

    def inner(i):
        for k in range(CORES):
            copies[k][i + 1].wait()
        value = fold_rows(dot_nt(weights, x_ref[pl.ds(i * rows, rows), :]), PIECES)
        inner_ref[:, pl.ds(i * rows, rows)] = pieces_of(value, PIECES)
        return value

    put_tiles(
        send_ref,
        passes(inner, lambda i: x_ref[pl.ds(i * rows, rows), half:], CHUNKS, acc_ref),
    )


def own_power_kernel(inner_ref, x_ref, keep_ref):
    half = x_ref.shape[1] // CORES
    power = jnp.dot(inner_ref[...], x_ref[:, :half], preferred_element_type=jnp.float32)
    put_tiles(keep_ref, fold_rows(power, PIECES))


def add_kernel(keep_ref, came_ref, out_ref):
    out_ref[...] = keep_ref[...] + came_ref[...]


def spread_kernel(parts_ref, out_ref):
    out_ref[...] = jnp.broadcast_to(jnp.sum(parts_ref[...], axis=0)[None], out_ref.shape)


def own_modes_kernel(x_ref, own_ref, modes_ref):
    half = x_ref.shape[1] // CORES
    weights = pieces_of(get_tiles(own_ref), PIECES)
    modes = jnp.dot(x_ref[:, :half], weights.T, preferred_element_type=jnp.float32)
    modes_ref[...] = fold_rows(modes.T, PIECES)


def coords_kernel(x_ref, own_modes_ref, other_ref, keep_ref, send_ref, modes_ref, acc_ref):
    half = x_ref.shape[1] // CORES
    rows = x_ref.shape[0] // BLOCKS
    weights = pieces_of(get_tiles(other_ref), PIECES).T

    def inner(i):
        here = pl.ds(i * rows, rows)
        value = jnp.dot(x_ref[here, half:], weights, preferred_element_type=jnp.float32)
        value = fold_rows(value.T, PIECES)
        value = own_modes_ref[:, here] + value
        modes_ref[:, here] = value
        return value

    coords = passes(inner, lambda i: x_ref[pl.ds(i * rows, rows), :], BLOCKS, acc_ref)
    first = lax.axis_index("core") == 0
    own, other = coords[:, :half], coords[:, half:]
    coords = jnp.concatenate([jnp.where(first, own, other), jnp.where(first, other, own)], axis=1)
    groups, deep, _ = keep_ref.shape
    span = deep - 8
    later = jnp.concatenate([coords[:, span:], coords[:, :span]], axis=1)
    coords = jnp.concatenate([coords, later], axis=0).T.reshape(groups, -1, 2 * RANK)
    packed = [coords[:, 2 * span * c : 2 * span * c + deep] for c in range(CORES)]
    keep_ref[...] = jnp.where(first, packed[0], packed[1])
    send_ref[...] = jnp.where(first, packed[1], packed[0])


def correlation_kernel(own_ref, other_ref, corr_ref):
    power = jnp.concatenate([get_tiles(own_ref), get_tiles(other_ref)], axis=1)
    pieces = pieces_of(power, 3)
    corr_ref[...] = fold_rows(fold_lanes(dot_nt(pieces, pieces), 3), 3)


def pair_kernel(keep_ref, came_ref, out_hbm, out_ref, sem):
    total = keep_ref[...] + came_ref[...]
    turned = pltpu.roll(total, RANK, axis=2)
    left = lax.broadcasted_iota(jnp.int32, (1, 1, 2 * RANK), 2) < RANK
    groups = total.shape[0]
    chips, deep = out_ref.shape[:2]
    slabs = chips // groups
    share = 2 * deep - 2
    for x in range(slabs):
        side, place = divmod(x * share, total.shape[1] - 8)
        near, far = (total, turned) if side == 0 else (turned, total)
        middle = place + deep
        chunk = jnp.where(left, near[:, place:middle], far[:, middle : middle + deep])
        for g in range(groups):
            for i in range(deep):
                out_ref[slabs * g + x, i] = chunk[g, i : i + 1]
    copy = pltpu.make_async_copy(out_ref, out_hbm, sem)
    copy.start()
    copy.wait()


def spread_lane(line, k):
    return jnp.broadcast_to(line[:, k : k + 1], line.shape)


def factor_kernel(
    corr_ref, modes_hbm, quad_hbm, projection_hbm, inverse_ref, pieces_ref,
    modes_ref, quad_ref, projection_ref, sems,
):
    quad_fetch = pltpu.make_async_copy(quad_hbm, quad_ref, sems.at[0])
    modes_fetch = pltpu.make_async_copy(modes_hbm, modes_ref, sems.at[1])
    quad_fetch.start()
    modes_fetch.start()
    row = lax.broadcasted_iota(jnp.int32, (RANK, RANK), 0)
    column = lax.broadcasted_iota(jnp.int32, (RANK, RANK), 1)
    unit = jnp.where(row == column, jnp.float32(1.0), jnp.float32(0.0))
    work = jnp.concatenate([corr_ref[...], unit], axis=1)
    index = lax.broadcasted_iota(jnp.int32, (RANK, 1), 0)
    top = 0
    for k in range(0, RANK, 2):
        first, second = work[k - top : k - top + 1], work[k - top + 1 : k - top + 2]
        pivot, cross = spread_lane(first, k), spread_lane(first, k + 1)
        inverse = 1.0 / pivot
        ratio = cross * inverse
        other = spread_lane(second, k + 1) - cross * ratio
        second = second - ratio * first
        inverse_ref[k : k + 1] = first[:, RANK:] * (1.0 / jnp.sqrt(pivot[:, RANK:]))
        inverse_ref[k + 1 : k + 2] = second[:, RANK:] * (1.0 / jnp.sqrt(other[:, RANK:]))
        if k + 2 == RANK:
            break
        place = (k + 2) // 8 * 8
        work = work[place - top :]
        top = place
        below = index[top:] > k + 1
        left = jnp.where(below, work[:, k : k + 1], 0.0)
        right = jnp.where(below, work[:, k + 1 : k + 2], 0.0)
        scaled = second * (1.0 / other)
        work = work - (left * (first * inverse - ratio * scaled) + right * scaled)
    quad_fetch.wait()
    pieces_ref[...] = pieces_of(quad_ref[...], PIECES).T
    modes_fetch.wait()
    left = pieces_of(inverse_ref[...], 3)
    modes = jnp.dot(
        jnp.concatenate([left] * 3, axis=1),
        pieces_of(modes_ref[...], 3),
        preferred_element_type=jnp.float32,
    )
    projection_ref[...] = fold_rows(modes, 3).astype(jnp.bfloat16)
    copy = pltpu.make_async_copy(projection_ref, projection_hbm, sems.at[2])
    copy.start()
    copy.wait()


def rollout_kernel(
    scale, width, parts_ref, inverse_ref, linear_ref, pieces_ref, offset_ref,
    reduced_hbm, mismatch_hbm, reduced_ref, mismatch_ref, sems,
):
    share = reduced_ref.shape[0]
    deep = share // 2 + 1
    run = 8 * deep
    total = sum(parts_ref[i : i + run, :] for i in range(0, parts_ref.shape[0], run))
    packed = sum(total[i : i + deep] for i in range(0, run, deep))
    coords = jnp.concatenate([packed[:, :RANK], packed[:, RANK:]], axis=0)
    coords = scale * lax.dot_general(
        coords,
        inverse_ref[...],
        NT,
        precision=lax.Precision.HIGHEST,
        preferred_element_type=jnp.float32,
    )
    state, target = coords[:share], coords[2:]
    reduced_ref[...] = state
    reduced_copy = pltpu.make_async_copy(reduced_ref, reduced_hbm, sems.at[0])
    reduced_copy.start()
    pieces = pieces_ref[...]
    upper = lax.broadcasted_iota(jnp.int32, (share, 2 * RANK), 1) >= RANK
    for _ in range(2):
        twice = jnp.concatenate([state, state], axis=1)
        pairs = jnp.concatenate(
            [
                jnp.where(upper, state[:, 2 * i + 1 : 2 * i + 2], state[:, 2 * i : 2 * i + 1])
                * twice
                for i in range(RANK // 2)
            ],
            axis=1,
        )
        quadratic = jnp.dot(
            pieces_of(pairs, PIECES), pieces, preferred_element_type=jnp.float32
        )
        quadratic = fold_rows(fold_lanes(quadratic, PIECES), PIECES)
        linear = jnp.dot(
            state,
            linear_ref[...],
            precision=lax.Precision.HIGHEST,
            preferred_element_type=jnp.float32,
        )
        state = state + 0.25 * (linear + quadratic + offset_ref[...])
    position = lax.axis_index(EVERY) * share + lax.broadcasted_iota(jnp.int32, (share, 1), 0)
    mismatch_ref[...] = jnp.where(position < width - 2, state - target, jnp.float32(0.0))
    mismatch_copy = pltpu.make_async_copy(mismatch_ref, mismatch_hbm, sems.at[1])
    mismatch_copy.start()
    reduced_copy.wait()
    mismatch_copy.wait()


def in_hbm(value):
    return pltpu.with_memory_space_constraint(value, pltpu.HBM)


def call(kernel, name, outs, ins, scratch=(), places=None):
    return pl.pallas_call(
        kernel,
        out_shape=outs,
        in_specs=ins,
        out_specs=places or jax.tree.map(lambda _: VMEM, outs),
        scratch_shapes=list(scratch),
        compiler_params=LIMIT,
        name=name,
    )


def body(snapshots, start_block, linear_op, quad_op, offset):
    devices = lax.axis_size(EVERY)
    rows, width = snapshots.shape
    share = width // devices
    f32 = jnp.float32
    shape = jax.ShapeDtypeStruct
    chips = devices // CORES
    tiles = shape((chips, RANK * share // 128, 128), f32)
    small = shape((RANK, RANK), f32)
    own = shape((share, RANK), f32)
    send, held, inner = call(
        power_kernel,
        "power",
        (
            tiles,
            shape((rows, width), jnp.bfloat16),
            shape((PIECES * RANK, rows), jnp.bfloat16),
        ),
        [HBM, HBM],
        [
            pltpu.VMEM((RANK, width), f32),
            pltpu.VMEM((PIECES * RANK, width // CORES), f32),
            pltpu.SemaphoreType.DMA((CORES, CHUNKS + 1)),
        ],
    )(in_hbm(snapshots), in_hbm(start_block.T))
    swap = [(0, 1), (1, 0)]
    came = lax.ppermute(send, "core", swap)
    keep = call(own_power_kernel, "own_power", tiles, [VMEM, VMEM])(inner, held)
    parts = call(add_kernel, "add", tiles, [VMEM, VMEM])(keep, came)
    parts = lax.all_to_all(parts, CHIPS, 0, 0, tiled=True)
    spread = call(spread_kernel, "spread", tiles, [VMEM])(parts)
    mine = lax.all_to_all(spread, CHIPS, 0, 0, tiled=True)
    theirs = lax.ppermute(mine, "core", swap)
    own_modes = call(own_modes_kernel, "own_modes", shape((RANK, rows), f32), [VMEM, VMEM])(
        held, mine
    )
    groups = lax.axis_size("yz")
    deep = width // groups // CORES // 2 + 8
    packed = shape((groups, deep, 2 * RANK), f32)
    keep, send, modes = call(
        coords_kernel,
        "coords",
        (packed, packed, shape((RANK, rows), f32)),
        [VMEM, VMEM, VMEM],
        [pltpu.VMEM((PIECES * RANK, width), f32)],
    )(held, own_modes, theirs)
    came = lax.ppermute(send, "core", swap)
    correlation = call(correlation_kernel, "correlation", small, [VMEM, VMEM])(mine, theirs)
    came, correlation = lax.optimization_barrier((came, correlation))
    chunk = (chips, share // 2 + 1, 1, 2 * RANK)
    parts = call(
        pair_kernel,
        "pair",
        shape(chunk, f32),
        [VMEM, VMEM],
        [pltpu.VMEM(chunk, f32), pltpu.SemaphoreType.DMA(())],
        HBM,
    )(keep, came)
    parts = lax.all_to_all(parts, CHIPS, 0, 0, tiled=True).reshape(-1, 2 * RANK)
    projection, inverse, pieces = call(
        factor_kernel,
        "factor",
        (
            shape((RANK, rows), jnp.bfloat16),
            small,
            shape((RANK * RANK, PIECES * RANK), jnp.bfloat16),
        ),
        [VMEM, HBM, HBM],
        [
            pltpu.VMEM((RANK, rows), f32),
            pltpu.VMEM((RANK, RANK * RANK), f32),
            pltpu.VMEM((RANK, rows), jnp.bfloat16),
            pltpu.SemaphoreType.DMA((3,)),
        ],
        (HBM, VMEM, VMEM),
    )(correlation, in_hbm(modes), in_hbm(quad_op.T))
    factor_scale = math.sqrt(width) / (rows * devices)
    reduced, mismatch = call(
        lambda *refs: rollout_kernel(factor_scale, width, *refs),
        "rollout",
        (own, own),
        [VMEM] * 5,
        [
            pltpu.VMEM((share, RANK), f32),
            pltpu.VMEM((share, RANK), f32),
            pltpu.SemaphoreType.DMA((2,)),
        ],
        (HBM, HBM),
    )(parts, inverse, linear_op, pieces, offset[None, :])
    return (projection.T, reduced, mismatch)


def solution(mesh):
    slabs = mesh.shape["slab"]
    split = Mesh(mesh.devices.reshape(-1, CORES, slabs), EVERY)
    whole = P(EVERY, None)
    return jax.shard_map(
        body,
        mesh=split,
        in_specs=(whole, P(), P(), P(), P()),
        out_specs=(whole, whole, whole),
        check_vma=False,
    )
```

```python
import math

import jax
import jax.numpy as jnp
from jax import lax
from jax.experimental import pallas as pl
from jax.experimental.pallas import tpu as pltpu
from jax.sharding import Mesh
from jax.sharding import PartitionSpec as P

EVERY = ("yz", "core", "slab")
CHIPS = ("yz", "slab")
CORES = 2
RANK = 64
CHUNKS = 4
BLOCKS = 2
PIECES = 2
NT = (((1,), (1,)), ((), ()))
LIMIT = pltpu.CompilerParams(vmem_limit_bytes=20 * 1024 * 1024)
VMEM = pl.BlockSpec(memory_space=pltpu.VMEM)
HBM = pl.BlockSpec(memory_space=pltpu.HBM)


def pieces_of(value, count, axis=0):
    pieces = []
    for _ in range(count):
        piece = value.astype(jnp.bfloat16)
        pieces.append(piece)
        value = value - piece.astype(jnp.float32)
    return jnp.concatenate(pieces, axis=axis)


def fold_rows(value, count):
    part = value.shape[0] // count
    return sum(value[i * part : (i + 1) * part] for i in range(count))


def fold_lanes(value, count):
    part = value.shape[1] // count
    return sum(value[:, i * part : (i + 1) * part] for i in range(count))


def dot_nt(left, right):
    return lax.dot_general(left, right, NT, preferred_element_type=jnp.float32)


def passes(inner, block, count, acc_ref):
    held = None
    for i in range(count):
        value = inner(i)
        if held is not None:
            part = jnp.dot(held, block(i - 1), preferred_element_type=jnp.float32)
            acc_ref[...] = part if i == 1 else acc_ref[...] + part
        held = pieces_of(value, PIECES)
    part = jnp.dot(held, block(count - 1), preferred_element_type=jnp.float32)
    return fold_rows(acc_ref[...] + part, PIECES)


def put_tiles(out_ref, value):
    wide = value.shape[1] // 128
    for i in range(out_ref.shape[0]):
        a, b = divmod(i, wide)
        out_ref[i] = value[8 * a : 8 * a + 8, 128 * b : 128 * b + 128]


def get_tiles(ref):
    tall = RANK // 8
    wide = ref.shape[0] // tall
    rows = [
        jnp.concatenate([ref[a * wide + b] for b in range(wide)], axis=1) for a in range(tall)
    ]
    return jnp.concatenate(rows, axis=0)


def power_kernel(x_hbm, start_hbm, send_ref, x_ref, inner_ref, start_ref, acc_ref, sems):
    half = x_ref.shape[1] // CORES
    rows = x_ref.shape[0] // CHUNKS
    copies = []
    for k in range(CORES):
        source = pl.multiple_of(half * jnp.bitwise_xor(lax.axis_index("core"), k), half)
        there, here = pl.ds(source, half), pl.ds(k * half, half)
        copies.append(
            [pltpu.make_async_copy(start_hbm.at[:, there], start_ref.at[:, here], sems.at[k, CHUNKS])]
            + [
                pltpu.make_async_copy(
                    x_hbm.at[pl.ds(i * rows, rows), there],
                    x_ref.at[pl.ds(i * rows, rows), here],
                    sems.at[k, i],
                )
                for i in range(CHUNKS)
            ]
        )
    for pair in zip(*copies):
        for copy in pair:
            copy.start()
    for k in range(CORES):
        copies[k][0].wait()
    weights = pieces_of(start_ref[...], PIECES)

    def inner(i):
        for k in range(CORES):
            copies[k][i + 1].wait()
        value = fold_rows(dot_nt(weights, x_ref[pl.ds(i * rows, rows), :]), PIECES)
        inner_ref[:, pl.ds(i * rows, rows)] = pieces_of(value, PIECES)
        return value

    put_tiles(
        send_ref,
        passes(inner, lambda i: x_ref[pl.ds(i * rows, rows), half:], CHUNKS, acc_ref),
    )


def own_power_kernel(inner_ref, x_ref, keep_ref):
    half = x_ref.shape[1] // CORES
    power = jnp.dot(inner_ref[...], x_ref[:, :half], preferred_element_type=jnp.float32)
    put_tiles(keep_ref, fold_rows(power, PIECES))


def add_kernel(keep_ref, came_ref, out_ref):
    out_ref[...] = keep_ref[...] + came_ref[...]


def spread_kernel(parts_ref, out_ref):
    out_ref[...] = jnp.broadcast_to(jnp.sum(parts_ref[...], axis=0)[None], out_ref.shape)


def own_modes_kernel(x_ref, own_ref, modes_ref):
    half = x_ref.shape[1] // CORES
    weights = pieces_of(get_tiles(own_ref), PIECES)
    modes = jnp.dot(x_ref[:, :half], weights.T, preferred_element_type=jnp.float32)
    modes_ref[...] = fold_rows(modes.T, PIECES)


def coords_kernel(x_ref, own_modes_ref, other_ref, keep_ref, send_ref, modes_ref, acc_ref):
    half = x_ref.shape[1] // CORES
    rows = x_ref.shape[0] // BLOCKS
    weights = pieces_of(get_tiles(other_ref), PIECES).T

    def inner(i):
        here = pl.ds(i * rows, rows)
        value = jnp.dot(x_ref[here, half:], weights, preferred_element_type=jnp.float32)
        value = fold_rows(value.T, PIECES)
        value = own_modes_ref[:, here] + value
        modes_ref[:, here] = value
        return value

    coords = passes(inner, lambda i: x_ref[pl.ds(i * rows, rows), :], BLOCKS, acc_ref)
    first = lax.axis_index("core") == 0
    own, other = coords[:, :half], coords[:, half:]
    coords = jnp.concatenate([jnp.where(first, own, other), jnp.where(first, other, own)], axis=1)
    groups, deep, _ = keep_ref.shape
    span = deep - 8
    later = jnp.concatenate([coords[:, span:], coords[:, :span]], axis=1)
    coords = jnp.concatenate([coords, later], axis=0).T.reshape(groups, -1, 2 * RANK)
    packed = [coords[:, 2 * span * c : 2 * span * c + deep] for c in range(CORES)]
    keep_ref[...] = jnp.where(first, packed[0], packed[1])
    send_ref[...] = jnp.where(first, packed[1], packed[0])


def correlation_kernel(own_ref, other_ref, corr_ref):
    power = jnp.concatenate([get_tiles(own_ref), get_tiles(other_ref)], axis=1)
    pieces = pieces_of(power, 3)
    corr_ref[...] = fold_rows(fold_lanes(dot_nt(pieces, pieces), 3), 3)


def pair_kernel(keep_ref, came_ref, out_hbm, out_ref, sems):
    total = keep_ref[...] + came_ref[...]
    turned = pltpu.roll(total, RANK, axis=2)
    left = lax.broadcasted_iota(jnp.int32, (1, 1, 2 * RANK), 2) < RANK
    groups = total.shape[0]
    chips, deep = out_ref.shape[:2]
    slabs = chips // groups
    share = 2 * deep - 2
    part = groups // 2
    copies = []
    for start in range(0, groups, part):
        for x in range(slabs):
            side, place = divmod(x * share, total.shape[1] - 8)
            near, far = (total, turned) if side == 0 else (turned, total)
            near, far = near[start : start + part], far[start : start + part]
            middle = place + deep
            chunk = jnp.where(left, near[:, place:middle], far[:, middle : middle + deep])
            for g in range(part):
                for i in range(deep):
                    out_ref[slabs * (start + g) + x, i] = chunk[g, i : i + 1]
        here = pl.ds(slabs * start, slabs * part)
        copies.append(
            pltpu.make_async_copy(out_ref.at[here], out_hbm.at[here], sems.at[start // part])
        )
        copies[-1].start()
    for copy in copies:
        copy.wait()


def spread_lane(line, k):
    return jnp.broadcast_to(line[:, k : k + 1], line.shape)


def factor_kernel(
    corr_ref, modes_hbm, quad_hbm, projection_hbm, inverse_ref, pieces_ref,
    modes_ref, quad_ref, projection_ref, sems,
):
    quad_fetch = pltpu.make_async_copy(quad_hbm, quad_ref, sems.at[0])
    modes_fetch = pltpu.make_async_copy(modes_hbm, modes_ref, sems.at[1])
    quad_fetch.start()
    modes_fetch.start()
    row = lax.broadcasted_iota(jnp.int32, (RANK, RANK), 0)
    column = lax.broadcasted_iota(jnp.int32, (RANK, RANK), 1)
    unit = jnp.where(row == column, jnp.float32(1.0), jnp.float32(0.0))
    work = jnp.concatenate([corr_ref[...], unit], axis=1)
    index = lax.broadcasted_iota(jnp.int32, (RANK, 1), 0)
    top = 0
    for k in range(0, RANK, 2):
        first, second = work[k - top : k - top + 1], work[k - top + 1 : k - top + 2]
        pivot, cross = spread_lane(first, k), spread_lane(first, k + 1)
        inverse = 1.0 / pivot
        ratio = cross * inverse
        other = spread_lane(second, k + 1) - cross * ratio
        second = second - ratio * first
        inverse_ref[k : k + 1] = first[:, RANK:] * (1.0 / jnp.sqrt(pivot[:, RANK:]))
        inverse_ref[k + 1 : k + 2] = second[:, RANK:] * (1.0 / jnp.sqrt(other[:, RANK:]))
        if k + 2 == RANK:
            break
        place = (k + 2) // 8 * 8
        work = work[place - top :]
        top = place
        below = index[top:] > k + 1
        left = jnp.where(below, work[:, k : k + 1], 0.0)
        right = jnp.where(below, work[:, k + 1 : k + 2], 0.0)
        scaled = second * (1.0 / other)
        work = work - (left * (first * inverse - ratio * scaled) + right * scaled)
    quad_fetch.wait()
    pieces_ref[...] = pieces_of(quad_ref[...], PIECES).T
    modes_fetch.wait()
    left = pieces_of(inverse_ref[...], 3)
    modes = jnp.dot(
        jnp.concatenate([left] * 3, axis=1),
        pieces_of(modes_ref[...], 3),
        preferred_element_type=jnp.float32,
    )
    projection_ref[...] = fold_rows(modes, 3).astype(jnp.bfloat16)
    copy = pltpu.make_async_copy(projection_ref, projection_hbm, sems.at[2])
    copy.start()
    copy.wait()


def rollout_kernel(
    scale, width, parts_ref, inverse_ref, linear_ref, pieces_ref, offset_ref,
    reduced_hbm, mismatch_hbm, reduced_ref, mismatch_ref, sems,
):
    share = reduced_ref.shape[0]
    deep = share // 2 + 1
    run = 8 * deep
    total = sum(parts_ref[i : i + run, :] for i in range(0, parts_ref.shape[0], run))
    packed = sum(total[i : i + deep] for i in range(0, run, deep))
    coords = jnp.concatenate([packed[:, :RANK], packed[:, RANK:]], axis=0)
    coords = scale * lax.dot_general(
        coords,
        inverse_ref[...],
        NT,
        precision=lax.Precision.HIGHEST,
        preferred_element_type=jnp.float32,
    )
    state, target = coords[:share], coords[2:]
    reduced_ref[...] = state
    reduced_copy = pltpu.make_async_copy(reduced_ref, reduced_hbm, sems.at[0])
    reduced_copy.start()
    pieces = pieces_ref[...]
    upper = lax.broadcasted_iota(jnp.int32, (share, 2 * RANK), 1) >= RANK
    for _ in range(2):
        twice = jnp.concatenate([state, state], axis=1)
        pairs = jnp.concatenate(
            [
                jnp.where(upper, state[:, 2 * i + 1 : 2 * i + 2], state[:, 2 * i : 2 * i + 1])
                * twice
                for i in range(RANK // 2)
            ],
            axis=1,
        )
        quadratic = jnp.dot(
            pieces_of(pairs, PIECES), pieces, preferred_element_type=jnp.float32
        )
        quadratic = fold_rows(fold_lanes(quadratic, PIECES), PIECES)
        linear = jnp.dot(
            state,
            linear_ref[...],
            precision=lax.Precision.HIGHEST,
            preferred_element_type=jnp.float32,
        )
        state = state + 0.25 * (linear + quadratic + offset_ref[...])
    position = lax.axis_index(EVERY) * share + lax.broadcasted_iota(jnp.int32, (share, 1), 0)
    mismatch_ref[...] = jnp.where(position < width - 2, state - target, jnp.float32(0.0))
    mismatch_copy = pltpu.make_async_copy(mismatch_ref, mismatch_hbm, sems.at[1])
    mismatch_copy.start()
    reduced_copy.wait()
    mismatch_copy.wait()


def in_hbm(value):
    return pltpu.with_memory_space_constraint(value, pltpu.HBM)


def call(kernel, name, outs, ins, scratch=(), places=None):
    return pl.pallas_call(
        kernel,
        out_shape=outs,
        in_specs=ins,
        out_specs=places or jax.tree.map(lambda _: VMEM, outs),
        scratch_shapes=list(scratch),
        compiler_params=LIMIT,
        name=name,
    )


def body(snapshots, start_block, linear_op, quad_op, offset):
    devices = lax.axis_size(EVERY)
    rows, width = snapshots.shape
    share = width // devices
    f32 = jnp.float32
    shape = jax.ShapeDtypeStruct
    chips = devices // CORES
    tiles = shape((chips, RANK * share // 128, 128), f32)
    small = shape((RANK, RANK), f32)
    own = shape((share, RANK), f32)
    send, held, inner = call(
        power_kernel,
        "power",
        (
            tiles,
            shape((rows, width), jnp.bfloat16),
            shape((PIECES * RANK, rows), jnp.bfloat16),
        ),
        [HBM, HBM],
        [
            pltpu.VMEM((RANK, width), f32),
            pltpu.VMEM((PIECES * RANK, width // CORES), f32),
            pltpu.SemaphoreType.DMA((CORES, CHUNKS + 1)),
        ],
    )(in_hbm(snapshots), in_hbm(start_block.T))
    swap = [(0, 1), (1, 0)]
    came = lax.ppermute(send, "core", swap)
    keep = call(own_power_kernel, "own_power", tiles, [VMEM, VMEM])(inner, held)
    parts = call(add_kernel, "add", tiles, [VMEM, VMEM])(keep, came)
    parts = lax.all_to_all(parts, CHIPS, 0, 0, tiled=True)
    spread = call(spread_kernel, "spread", tiles, [VMEM])(parts)
    mine = lax.all_to_all(spread, CHIPS, 0, 0, tiled=True)
    theirs = lax.ppermute(mine, "core", swap)
    own_modes = call(own_modes_kernel, "own_modes", shape((RANK, rows), f32), [VMEM, VMEM])(
        held, mine
    )
    groups = lax.axis_size("yz")
    deep = width // groups // CORES // 2 + 8
    packed = shape((groups, deep, 2 * RANK), f32)
    keep, send, modes = call(
        coords_kernel,
        "coords",
        (packed, packed, shape((RANK, rows), f32)),
        [VMEM, VMEM, VMEM],
        [pltpu.VMEM((PIECES * RANK, width), f32)],
    )(held, own_modes, theirs)
    came = lax.ppermute(send, "core", swap)
    correlation = call(correlation_kernel, "correlation", small, [VMEM, VMEM])(mine, theirs)
    came, correlation = lax.optimization_barrier((came, correlation))
    chunk = (chips, share // 2 + 1, 1, 2 * RANK)
    parts = call(
        pair_kernel,
        "pair",
        shape(chunk, f32),
        [VMEM, VMEM],
        [pltpu.VMEM(chunk, f32), pltpu.SemaphoreType.DMA((2,))],
        HBM,
    )(keep, came)
    parts = lax.all_to_all(parts, CHIPS, 0, 0, tiled=True).reshape(-1, 2 * RANK)
    projection, inverse, pieces = call(
        factor_kernel,
        "factor",
        (
            shape((RANK, rows), jnp.bfloat16),
            small,
            shape((RANK * RANK, PIECES * RANK), jnp.bfloat16),
        ),
        [VMEM, HBM, HBM],
        [
            pltpu.VMEM((RANK, rows), f32),
            pltpu.VMEM((RANK, RANK * RANK), f32),
            pltpu.VMEM((RANK, rows), jnp.bfloat16),
            pltpu.SemaphoreType.DMA((3,)),
        ],
        (HBM, VMEM, VMEM),
    )(correlation, in_hbm(modes), in_hbm(quad_op.T))
    factor_scale = math.sqrt(width) / (rows * devices)
    reduced, mismatch = call(
        lambda *refs: rollout_kernel(factor_scale, width, *refs),
        "rollout",
        (own, own),
        [VMEM] * 5,
        [
            pltpu.VMEM((share, RANK), f32),
            pltpu.VMEM((share, RANK), f32),
            pltpu.SemaphoreType.DMA((2,)),
        ],
        (HBM, HBM),
    )(parts, inverse, linear_op, pieces, offset[None, :])
    return (projection.T, reduced, mismatch)


def solution(mesh):
    slabs = mesh.shape["slab"]
    split = Mesh(mesh.devices.reshape(-1, CORES, slabs), EVERY)
    whole = P(EVERY, None)
    return jax.shard_map(
        body,
        mesh=split,
        in_specs=(whole, P(), P(), P(), P()),
        out_specs=(whole, whole, whole),
        check_vma=False,
    )
```

```python
import math

import jax
import jax.numpy as jnp
from jax import lax
from jax.experimental import pallas as pl
from jax.experimental.pallas import tpu as pltpu
from jax.sharding import Mesh
from jax.sharding import PartitionSpec as P

EVERY = ("yz", "core", "slab")
CHIPS = ("yz", "slab")
CORES = 2
RANK = 64
CHUNKS = 4
BLOCKS = 2
PIECES = 2
NT = (((1,), (1,)), ((), ()))
LIMIT = pltpu.CompilerParams(vmem_limit_bytes=20 * 1024 * 1024)
VMEM = pl.BlockSpec(memory_space=pltpu.VMEM)
HBM = pl.BlockSpec(memory_space=pltpu.HBM)


def pieces_of(value, count, axis=0):
    pieces = []
    for _ in range(count):
        piece = value.astype(jnp.bfloat16)
        pieces.append(piece)
        value = value - piece.astype(jnp.float32)
    return jnp.concatenate(pieces, axis=axis)


def fold_rows(value, count):
    part = value.shape[0] // count
    return sum(value[i * part : (i + 1) * part] for i in range(count))


def fold_lanes(value, count):
    part = value.shape[1] // count
    return sum(value[:, i * part : (i + 1) * part] for i in range(count))


def dot_nt(left, right):
    return lax.dot_general(left, right, NT, preferred_element_type=jnp.float32)


def passes(inner, block, count, acc_ref):
    held = None
    for i in range(count):
        value = inner(i)
        if held is not None:
            part = jnp.dot(held, block(i - 1), preferred_element_type=jnp.float32)
            total = part if i == 1 else total + part
        held = pieces_of(value, PIECES)
    part = jnp.dot(held, block(count - 1), preferred_element_type=jnp.float32)
    return fold_rows(total + part, PIECES)


def put_tiles(out_ref, value):
    wide = value.shape[1] // 128
    for i in range(out_ref.shape[0]):
        a, b = divmod(i, wide)
        out_ref[i] = value[8 * a : 8 * a + 8, 128 * b : 128 * b + 128]


def get_tiles(ref):
    tall = RANK // 8
    wide = ref.shape[0] // tall
    rows = [
        jnp.concatenate([ref[a * wide + b] for b in range(wide)], axis=1) for a in range(tall)
    ]
    return jnp.concatenate(rows, axis=0)


def power_kernel(x_hbm, start_hbm, send_ref, x_ref, inner_ref, start_ref, acc_ref, sems):
    half = x_ref.shape[1] // CORES
    rows = x_ref.shape[0] // CHUNKS
    copies = []
    for k in range(CORES):
        source = pl.multiple_of(half * jnp.bitwise_xor(lax.axis_index("core"), k), half)
        there, here = pl.ds(source, half), pl.ds(k * half, half)
        copies.append(
            [pltpu.make_async_copy(start_hbm.at[:, there], start_ref.at[:, here], sems.at[k, CHUNKS])]
            + [
                pltpu.make_async_copy(
                    x_hbm.at[pl.ds(i * rows, rows), there],
                    x_ref.at[pl.ds(i * rows, rows), here],
                    sems.at[k, i],
                )
                for i in range(CHUNKS)
            ]
        )
    for pair in zip(*copies):
        for copy in pair:
            copy.start()
    for k in range(CORES):
        copies[k][0].wait()
    weights = pieces_of(start_ref[...], PIECES)

    def inner(i):
        for k in range(CORES):
            copies[k][i + 1].wait()
        value = fold_rows(dot_nt(weights, x_ref[pl.ds(i * rows, rows), :]), PIECES)
        inner_ref[:, pl.ds(i * rows, rows)] = pieces_of(value, PIECES)
        return value

    put_tiles(
        send_ref,
        passes(inner, lambda i: x_ref[pl.ds(i * rows, rows), half:], CHUNKS, acc_ref),
    )


def own_power_kernel(inner_ref, x_ref, keep_ref):
    half = x_ref.shape[1] // CORES
    power = jnp.dot(inner_ref[...], x_ref[:, :half], preferred_element_type=jnp.float32)
    put_tiles(keep_ref, fold_rows(power, PIECES))


def add_kernel(keep_ref, came_ref, out_ref):
    out_ref[...] = keep_ref[...] + came_ref[...]


def spread_kernel(parts_ref, out_ref):
    out_ref[...] = jnp.broadcast_to(jnp.sum(parts_ref[...], axis=0)[None], out_ref.shape)


def own_modes_kernel(x_ref, own_ref, modes_ref):
    half = x_ref.shape[1] // CORES
    weights = pieces_of(get_tiles(own_ref), PIECES)
    modes = jnp.dot(x_ref[:, :half], weights.T, preferred_element_type=jnp.float32)
    modes_ref[...] = fold_rows(modes.T, PIECES)


def coords_kernel(x_ref, own_modes_ref, other_ref, keep_ref, send_ref, modes_ref, acc_ref):
    half = x_ref.shape[1] // CORES
    rows = x_ref.shape[0] // BLOCKS
    weights = pieces_of(get_tiles(other_ref), PIECES).T

    def inner(i):
        here = pl.ds(i * rows, rows)
        value = jnp.dot(x_ref[here, half:], weights, preferred_element_type=jnp.float32)
        value = fold_rows(value.T, PIECES)
        value = own_modes_ref[:, here] + value
        modes_ref[:, here] = value
        return value

    coords = passes(inner, lambda i: x_ref[pl.ds(i * rows, rows), :], BLOCKS, acc_ref)
    first = lax.axis_index("core") == 0
    own, other = coords[:, :half], coords[:, half:]
    coords = jnp.concatenate([jnp.where(first, own, other), jnp.where(first, other, own)], axis=1)
    groups, deep, _ = keep_ref.shape
    span = deep - 8
    later = jnp.concatenate([coords[:, span:], coords[:, :span]], axis=1)
    coords = jnp.concatenate([coords, later], axis=0).T.reshape(groups, -1, 2 * RANK)
    packed = [coords[:, 2 * span * c : 2 * span * c + deep] for c in range(CORES)]
    keep_ref[...] = jnp.where(first, packed[0], packed[1])
    send_ref[...] = jnp.where(first, packed[1], packed[0])


def correlation_kernel(own_ref, other_ref, corr_ref):
    power = jnp.concatenate([get_tiles(own_ref), get_tiles(other_ref)], axis=1)
    pieces = pieces_of(power, 3)
    corr_ref[...] = fold_rows(fold_lanes(dot_nt(pieces, pieces), 3), 3)


def pair_kernel(keep_ref, came_ref, out_hbm, out_ref, sems):
    total = keep_ref[...] + came_ref[...]
    turned = pltpu.roll(total, RANK, axis=2)
    left = lax.broadcasted_iota(jnp.int32, (1, 1, 2 * RANK), 2) < RANK
    groups = total.shape[0]
    chips, deep = out_ref.shape[:2]
    slabs = chips // groups
    share = 2 * deep - 2
    part = groups // 2
    copies = []
    for start in range(0, groups, part):
        for x in range(slabs):
            side, place = divmod(x * share, total.shape[1] - 8)
            near, far = (total, turned) if side == 0 else (turned, total)
            near, far = near[start : start + part], far[start : start + part]
            middle = place + deep
            chunk = jnp.where(left, near[:, place:middle], far[:, middle : middle + deep])
            for g in range(part):
                for i in range(deep):
                    out_ref[slabs * (start + g) + x, i] = chunk[g, i : i + 1]
        here = pl.ds(slabs * start, slabs * part)
        copies.append(
            pltpu.make_async_copy(out_ref.at[here], out_hbm.at[here], sems.at[start // part])
        )
        copies[-1].start()
    for copy in copies:
        copy.wait()


def spread_lane(line, k):
    return jnp.broadcast_to(line[:, k : k + 1], line.shape)


def factor_kernel(
    corr_ref, modes_hbm, quad_hbm, projection_hbm, inverse_ref, pieces_ref,
    modes_ref, quad_ref, projection_ref, sems,
):
    quad_fetch = pltpu.make_async_copy(quad_hbm, quad_ref, sems.at[0])
    modes_fetch = pltpu.make_async_copy(modes_hbm, modes_ref, sems.at[1])
    quad_fetch.start()
    modes_fetch.start()
    row = lax.broadcasted_iota(jnp.int32, (RANK, RANK), 0)
    column = lax.broadcasted_iota(jnp.int32, (RANK, RANK), 1)
    unit = jnp.where(row == column, jnp.float32(1.0), jnp.float32(0.0))
    work = jnp.concatenate([corr_ref[...], unit], axis=1)
    index = lax.broadcasted_iota(jnp.int32, (RANK, 1), 0)
    top = 0
    for k in range(0, RANK, 2):
        first, second = work[k - top : k - top + 1], work[k - top + 1 : k - top + 2]
        pivot, cross = spread_lane(first, k), spread_lane(first, k + 1)
        inverse = 1.0 / pivot
        ratio = cross * inverse
        other = spread_lane(second, k + 1) - cross * ratio
        second = second - ratio * first
        inverse_ref[k : k + 1] = first[:, RANK:] * (1.0 / jnp.sqrt(pivot[:, RANK:]))
        inverse_ref[k + 1 : k + 2] = second[:, RANK:] * (1.0 / jnp.sqrt(other[:, RANK:]))
        if k + 2 == RANK:
            break
        place = (k + 2) // 8 * 8
        work = work[place - top :]
        top = place
        below = index[top:] > k + 1
        left = jnp.where(below, work[:, k : k + 1], 0.0)
        right = jnp.where(below, work[:, k + 1 : k + 2], 0.0)
        scaled = second * (1.0 / other)
        work = work - (left * (first * inverse - ratio * scaled) + right * scaled)
    quad_fetch.wait()
    pieces_ref[...] = pieces_of(quad_ref[...], PIECES).T
    modes_fetch.wait()
    left = pieces_of(inverse_ref[...], 3)
    modes = jnp.dot(
        jnp.concatenate([left] * 3, axis=1),
        pieces_of(modes_ref[...], 3),
        preferred_element_type=jnp.float32,
    )
    projection_ref[...] = fold_rows(modes, 3).astype(jnp.bfloat16)
    copy = pltpu.make_async_copy(projection_ref, projection_hbm, sems.at[2])
    copy.start()
    copy.wait()


def rollout_kernel(
    scale, width, parts_ref, inverse_ref, linear_ref, pieces_ref, offset_ref,
    reduced_hbm, mismatch_hbm, reduced_ref, mismatch_ref, sems,
):
    share = reduced_ref.shape[0]
    deep = share // 2 + 1
    run = 8 * deep
    total = sum(parts_ref[i : i + run, :] for i in range(0, parts_ref.shape[0], run))
    packed = sum(total[i : i + deep] for i in range(0, run, deep))
    coords = jnp.concatenate([packed[:, :RANK], packed[:, RANK:]], axis=0)
    coords = scale * lax.dot_general(
        coords,
        inverse_ref[...],
        NT,
        precision=lax.Precision.HIGHEST,
        preferred_element_type=jnp.float32,
    )
    state, target = coords[:share], coords[2:]
    reduced_ref[...] = state
    reduced_copy = pltpu.make_async_copy(reduced_ref, reduced_hbm, sems.at[0])
    reduced_copy.start()
    pieces = pieces_ref[...]
    upper = lax.broadcasted_iota(jnp.int32, (share, 2 * RANK), 1) >= RANK
    for _ in range(2):
        twice = jnp.concatenate([state, state], axis=1)
        pairs = jnp.concatenate(
            [
                jnp.where(upper, state[:, 2 * i + 1 : 2 * i + 2], state[:, 2 * i : 2 * i + 1])
                * twice
                for i in range(RANK // 2)
            ],
            axis=1,
        )
        quadratic = jnp.dot(
            pieces_of(pairs, PIECES), pieces, preferred_element_type=jnp.float32
        )
        quadratic = fold_rows(fold_lanes(quadratic, PIECES), PIECES)
        linear = jnp.dot(
            state,
            linear_ref[...],
            precision=lax.Precision.HIGHEST,
            preferred_element_type=jnp.float32,
        )
        state = state + 0.25 * (linear + quadratic + offset_ref[...])
    position = lax.axis_index(EVERY) * share + lax.broadcasted_iota(jnp.int32, (share, 1), 0)
    mismatch_ref[...] = jnp.where(position < width - 2, state - target, jnp.float32(0.0))
    mismatch_copy = pltpu.make_async_copy(mismatch_ref, mismatch_hbm, sems.at[1])
    mismatch_copy.start()
    reduced_copy.wait()
    mismatch_copy.wait()


def in_hbm(value):
    return pltpu.with_memory_space_constraint(value, pltpu.HBM)


def call(kernel, name, outs, ins, scratch=(), places=None):
    return pl.pallas_call(
        kernel,
        out_shape=outs,
        in_specs=ins,
        out_specs=places or jax.tree.map(lambda _: VMEM, outs),
        scratch_shapes=list(scratch),
        compiler_params=LIMIT,
        name=name,
    )


def body(snapshots, start_block, linear_op, quad_op, offset):
    devices = lax.axis_size(EVERY)
    rows, width = snapshots.shape
    share = width // devices
    f32 = jnp.float32
    shape = jax.ShapeDtypeStruct
    chips = devices // CORES
    tiles = shape((chips, RANK * share // 128, 128), f32)
    small = shape((RANK, RANK), f32)
    own = shape((share, RANK), f32)
    send, held, inner = call(
        power_kernel,
        "power",
        (
            tiles,
            shape((rows, width), jnp.bfloat16),
            shape((PIECES * RANK, rows), jnp.bfloat16),
        ),
        [HBM, HBM],
        [
            pltpu.VMEM((RANK, width), f32),
            pltpu.VMEM((PIECES * RANK, width // CORES), f32),
            pltpu.SemaphoreType.DMA((CORES, CHUNKS + 1)),
        ],
    )(in_hbm(snapshots), in_hbm(start_block.T))
    swap = [(0, 1), (1, 0)]
    came = lax.ppermute(send, "core", swap)
    keep = call(own_power_kernel, "own_power", tiles, [VMEM, VMEM])(inner, held)
    parts = call(add_kernel, "add", tiles, [VMEM, VMEM])(keep, came)
    parts = lax.all_to_all(parts, CHIPS, 0, 0, tiled=True)
    spread = call(spread_kernel, "spread", tiles, [VMEM])(parts)
    mine = lax.all_to_all(spread, CHIPS, 0, 0, tiled=True)
    theirs = lax.ppermute(mine, "core", swap)
    own_modes = call(own_modes_kernel, "own_modes", shape((RANK, rows), f32), [VMEM, VMEM])(
        held, mine
    )
    groups = lax.axis_size("yz")
    deep = width // groups // CORES // 2 + 8
    packed = shape((groups, deep, 2 * RANK), f32)
    keep, send, modes = call(
        coords_kernel,
        "coords",
        (packed, packed, shape((RANK, rows), f32)),
        [VMEM, VMEM, VMEM],
        [pltpu.VMEM((PIECES * RANK, width), f32)],
    )(held, own_modes, theirs)
    came = lax.ppermute(send, "core", swap)
    correlation = call(correlation_kernel, "correlation", small, [VMEM, VMEM])(mine, theirs)
    came, correlation = lax.optimization_barrier((came, correlation))
    chunk = (chips, share // 2 + 1, 1, 2 * RANK)
    parts = call(
        pair_kernel,
        "pair",
        shape(chunk, f32),
        [VMEM, VMEM],
        [pltpu.VMEM(chunk, f32), pltpu.SemaphoreType.DMA((2,))],
        HBM,
    )(keep, came)
    parts = lax.all_to_all(parts, CHIPS, 0, 0, tiled=True).reshape(-1, 2 * RANK)
    projection, inverse, pieces = call(
        factor_kernel,
        "factor",
        (
            shape((RANK, rows), jnp.bfloat16),
            small,
            shape((RANK * RANK, PIECES * RANK), jnp.bfloat16),
        ),
        [VMEM, HBM, HBM],
        [
            pltpu.VMEM((RANK, rows), f32),
            pltpu.VMEM((RANK, RANK * RANK), f32),
            pltpu.VMEM((RANK, rows), jnp.bfloat16),
            pltpu.SemaphoreType.DMA((3,)),
        ],
        (HBM, VMEM, VMEM),
    )(correlation, in_hbm(modes), in_hbm(quad_op.T))
    factor_scale = math.sqrt(width) / (rows * devices)
    reduced, mismatch = call(
        lambda *refs: rollout_kernel(factor_scale, width, *refs),
        "rollout",
        (own, own),
        [VMEM] * 5,
        [
            pltpu.VMEM((share, RANK), f32),
            pltpu.VMEM((share, RANK), f32),
            pltpu.SemaphoreType.DMA((2,)),
        ],
        (HBM, HBM),
    )(parts, inverse, linear_op, pieces, offset[None, :])
    return (projection.T, reduced, mismatch)


def solution(mesh):
    slabs = mesh.shape["slab"]
    split = Mesh(mesh.devices.reshape(-1, CORES, slabs), EVERY)
    whole = P(EVERY, None)
    return jax.shard_map(
        body,
        mesh=split,
        in_specs=(whole, P(), P(), P(), P()),
        out_specs=(whole, whole, whole),
        check_vma=False,
    )
```
